512 devices in a mesh: rep: 32 (over z, core), exp: 16 (over y, x).
Axes of the slice: x: 4, y: 4, z: 16, core: 2. Of those that a mesh axis runs over, the one named last changes fastest.
Arguments:
- tokens: bfloat16 [65536, 4096], P(('rep', 'exp')), may hold values from -6 to 6
- grad_out: bfloat16 [65536, 4096], P(('rep', 'exp')), may hold values from -6 to 6
- gates: float32 [65536, 2], P(('rep', 'exp')), may hold values from 0.1 to 0.9
- expert_ids: int32 [65536, 2], P(('rep', 'exp')), may hold values from 0 to 15, all different within a row; in each aligned block of 128 rows (0 to 127, 128 to 255, ...) at most 20 rows name the same one
- w_all: bfloat16 [16, 4096, 384], P('exp', 'rep'), may hold values from -0.09375 to 0.09375
- touched: int32 [32, 16, 32], P('rep', 'exp'), may hold values 0 or 1
Outputs:
- token_grad: bfloat16 [65536, 4096], P(('rep', 'exp'))
- weight_grad: float32 [16, 4096, 384], P('exp', 'rep')
The draws below stay inside these ranges and needn't reach their ends.
Inputs may be any that keep to these rules, and one draw needn't show every extreme that they name: `expert_ids`: each token names two different experts. Among the tokens of one device no expert is named more than 20 times, a bound that some block reaches.
All inputs are finite; a program needn't handle non-finite values. No bound on the sum of `touched` on one device may be relied on, other than what follows from the above.
Results may differ from the reference program's by a relative error of at most 0.017.
Values may be sent and summed in bfloat16 or wider, within the bound.
No kernel may reach another device: no remote copies, remote signals or barrier semaphores. Data moves between devices by JAX's collectives and lax.ppermute only.
A program may use at most 64 MiB of HBM per device.

```python
import math
import jax
import jax.numpy as jnp
import numpy as np
from jax import lax

D = 4096
HID = 128
TOK_DEV = 128
EXPERTS = 16
CAP = 20
NB = 32
TOKENS = 65536
N_REP = 32
N_EXP = 16


def with_ends(array, stream_key, smallest, top_value):
    place = [jax.random.randint(jax.random.fold_in(stream_key, axis), (), 0, length) for axis, length in enumerate(array.shape)]
    widest = array.shape.index(max(array.shape))
    neighbour = place[:widest] + [(place[widest] + 1) % array.shape[widest]] + place[widest + 1:]
    return array.at[tuple(place)].set(smallest).at[tuple(neighbour)].set(top_value)


def shard_levels(key, extent, shards, smallest, high):
    def one(dim, blocks):
        steps = jax.random.uniform(jax.random.fold_in(jax.random.fold_in(key, 6), dim), (blocks,), jnp.float32, smallest / len(shards), high / len(shards))
        return jnp.repeat(jnp.exp(steps), extent[dim] // blocks).reshape((-1,) + (1,) * (len(extent) - dim - 1))

    level = one(*shards[0])
    for cut in shards[1:]:
        level = level * one(*cut)
    return level


def routed_block(own_key, own, number, rows, count, top, limit, lean):
    sequence = jax.random.permutation(own_key, count)
    crowded, ordinary = portions_of(count, rows * top, limit, lean, True), portions_of(count, rows * top, limit, lean, False)
    places = jnp.arange(count)

    def named(sizes, turn):
        used = int((sizes > 0).sum())
        fixed = max(1, used // 4)
        passed = fixed + (places - fixed + turn * (used - fixed)) % max(1, count - fixed)
        return jnp.zeros((count,), jnp.int32).at[sequence[jnp.where(places < fixed, places, passed)]].set(jnp.asarray(sizes, jnp.int32))

    sizes = jnp.where(number % 4 == 0, named(crowded, number // 4), named(ordinary, number - number // 4 - 1))
    mixed = jax.random.permutation(jax.random.fold_in(own, 3), count)
    giver, taker = mixed[0:count // 2 * 2:2], mixed[1:count // 2 * 2:2]
    margin = jnp.minimum(sizes[giver] - 1, limit - sizes[taker]) // 2
    margin = jnp.where((giver == sequence[0]) | (taker == sequence[0]) | (sizes[taker] == 0), 0, jnp.maximum(margin, 0))
    passed = jax.random.randint(jax.random.fold_in(own, 4), (count // 2,), 0, 1 << 20) % (margin + 1)
    sizes = sizes.at[giver].add(-passed).at[taker].add(passed)
    items = jnp.searchsorted(jnp.cumsum(sizes), jnp.arange(rows * top), side="right").astype(jnp.int32)
    listing = items.reshape(top, rows).T
    listing = listing[jax.random.permutation(jax.random.fold_in(own, 1), rows)]
    turn = jax.random.randint(jax.random.fold_in(own, 2), (rows, 1), 0, top)
    return jnp.take_along_axis(listing, (jnp.arange(top)[None, :] + turn) % top, axis=1)


def portions_of(amount, total, reach, lean, full):
    weights = [(1 << 20) // math.isqrt(rank ** lean) + 1 for rank in range(1, amount + 1)]
    largest = reach if full else min(reach, max(-(-total // amount), total * weights[0] // sum(weights)))
    least = 1 if total - largest >= amount - 1 else 0
    counts, rest = [largest] + [least] * (amount - 1), total - largest - least * (amount - 1)
    while rest > 0:
        candidates = [i for i in range(1, amount) if counts[i] < largest] or [i for i in range(1, amount) if counts[i] < reach]
        whole, remaining = sum([weights[i] for i in candidates]), rest
        for i in candidates:
            more = min(reach - counts[i], max(1, remaining * weights[i] // whole), rest)
            counts[i] = counts[i] + more
            rest = rest - more
    return np.array(counts)


def bell_draw(key, shape, width, bound, pieces=(), kind=jnp.bfloat16):
    loudness = shard_levels(key, shape, pieces, -0.22, 0.18) if pieces else 1.0
    entries = jax.random.normal(key, shape, jnp.float32) * width * loudness
    return jnp.minimum(jnp.maximum(entries, -bound), bound).astype(kind)


def setup_inputs(seed: int = 0) -> dict:
    key_list = jax.random.split(jax.random.key(seed), 7)
    tokens = bell_draw(key_list[0], (TOKENS, D), 1.0, 6.0, ((0, 512),))
    grad_out = bell_draw(key_list[1], (TOKENS, D), 1.0, 6.0, ((0, 512),))
    gates = jnp.clip(0.1 + 0.79999997 * jax.random.uniform(key_list[2], (TOKENS, 2), jnp.float32) ** shard_levels(key_list[2], (TOKENS, 2), ((0, 512),), -0.2, 0.2), 0.1, 0.9)
    expert_ids_keys = jax.random.split(jax.random.fold_in(key_list[3], 1), TOKENS // TOK_DEV)
    expert_ids_turns = jax.random.permutation(jax.random.fold_in(key_list[3], 3), TOKENS // TOK_DEV)
    expert_ids = jax.vmap(lambda own, number: routed_block(jax.random.fold_in(key_list[3], 2), own, number, TOK_DEV, EXPERTS, 2, CAP, 1))(expert_ids_keys, expert_ids_turns).reshape((TOKENS, 2))
    w_all = bell_draw(key_list[4], (EXPERTS, D, 3 * HID), D ** -0.5, 0.09375, ((0, 16), (1, 32)))
    touched = with_ends((jax.random.randint(key_list[5], (N_REP, EXPERTS, NB), 0, 2) < 1).astype(jnp.int32), jax.random.fold_in(key_list[5], 1), 0, 1)
    return {"tokens": tokens, "grad_out": grad_out, "gates": gates, "expert_ids": expert_ids, "w_all": w_all, "touched": touched}


def silu_terms(gate_pre):
    sigmoid_g = jax.nn.sigmoid(gate_pre)
    return gate_pre * sigmoid_g, sigmoid_g * (1.0 + gate_pre * (1.0 - sigmoid_g))


def expert_backward(slot_x, slot_dy, weights):
    hidden_count = weights.shape[1] // 3
    gate_up = jnp.dot(slot_x, weights[:, :2 * hidden_count], preferred_element_type=jnp.float32)
    hid_grad = jnp.dot(slot_dy, weights[:, 2 * hidden_count:], preferred_element_type=jnp.float32)
    gate_pre = gate_up[:, :hidden_count]
    up_pre = gate_up[:, hidden_count:]
    silu_val, silu_slope = silu_terms(gate_pre)
    hidden = (silu_val * up_pre).astype(jnp.bfloat16)
    gate_grad = (hid_grad * up_pre * silu_slope).astype(jnp.bfloat16)
    up_grad = (hid_grad * silu_val).astype(jnp.bfloat16)
    both_grad = jnp.concatenate([gate_grad, up_grad], 1)
    proj_grad = lax.dot_general(slot_x, both_grad, (((0,), (0,)), ((), ())), preferred_element_type=jnp.float32)
    down_grad = lax.dot_general(slot_dy, hidden, (((0,), (0,)), ((), ())), preferred_element_type=jnp.float32)
    full_grad = jnp.concatenate([proj_grad, down_grad], 1)
    slot_dx = lax.dot_general(both_grad, weights[:, :2 * hidden_count], (((1,), (1,)), ((), ())), preferred_element_type=jnp.float32)
    return full_grad, slot_dx.astype(jnp.bfloat16)


def reference(tokens, grad_out, gates, expert_ids, w_all, touched):
    capacity = 5 * TOK_DEV // (2 * EXPERTS)
    group_tokens = N_EXP * TOK_DEV
    slot_total = N_EXP * capacity

    def one_replica(grad_sum, replica):
        first = replica * group_tokens
        x_rep = lax.dynamic_slice_in_dim(tokens, first, group_tokens, 0)
        dy_rep = lax.dynamic_slice_in_dim(grad_out, first, group_tokens, 0)
        gate_rep = lax.dynamic_slice_in_dim(gates, first, group_tokens, 0)
        id_rep = lax.dynamic_slice_in_dim(expert_ids, first, group_tokens, 0)
        flat_ids = id_rep.reshape(N_EXP, 2 * TOK_DEV)
        onehot = (flat_ids[:, :, None] == jnp.arange(EXPERTS, dtype=jnp.int32)[None, None, :]).astype(jnp.int32)
        slot_rank = jnp.sum(jnp.cumsum(onehot, 1) * onehot, 2) - 1
        source = jnp.arange(N_EXP, dtype=jnp.int32)[:, None]
        slot_index = (flat_ids * slot_total + source * capacity + slot_rank).astype(jnp.int32)
        pair_index = jnp.arange(2 * group_tokens, dtype=jnp.int32)
        pair_table = jnp.full((EXPERTS * slot_total,), 2 * group_tokens, jnp.int32)
        pair_table = pair_table.at[slot_index.reshape(-1)].set(pair_index)
        token_table = (pair_table // 2).astype(jnp.int32)
        x_aug = jnp.concatenate([x_rep, jnp.zeros((1, D), jnp.bfloat16)], 0)
        scaled = (dy_rep.astype(jnp.float32)[:, None, :] * gate_rep[:, :, None]).astype(jnp.bfloat16)
        dy_aug = jnp.concatenate([scaled.reshape(2 * group_tokens, D), jnp.zeros((1, D), jnp.bfloat16)], 0)

        def one_expert(expert):
            pair_rows = lax.dynamic_slice_in_dim(pair_table, expert * slot_total, slot_total, 0)
            slot_x = x_aug[pair_rows // 2]
            slot_dy = dy_aug[pair_rows]
            full_grad, slot_dx = expert_backward(slot_x, slot_dy, w_all[expert])
            row_mask = jnp.repeat(touched[replica, expert].astype(jnp.float32), 128)[:, None]
            masked = lax.optimization_barrier((full_grad * row_mask).astype(jnp.bfloat16))
            return masked.astype(jnp.float32), slot_dx

        grads, slot_dxs = lax.map(one_expert, jnp.arange(EXPERTS, dtype=jnp.int32))
        token_sum = jnp.zeros((group_tokens + 1, D), jnp.float32)
        token_sum = token_sum.at[token_table].add(slot_dxs.reshape(-1, D).astype(jnp.float32))
        return grad_sum + grads, token_sum[:group_tokens].astype(jnp.bfloat16)

    start_sum = jnp.zeros((EXPERTS, D, 3 * HID), jnp.float32)
    grad_sum, token_grads = lax.scan(one_replica, start_sum, jnp.arange(N_REP, dtype=jnp.int32))
    return token_grads.reshape(N_REP * group_tokens, D), grad_sum
```

```python
import functools

import jax
import jax.numpy as jnp
from jax import lax
from jax.experimental import pallas as pl
from jax.experimental.pallas import tpu as pltpu
from jax.sharding import PartitionSpec as P

BF16 = jnp.bfloat16
F32 = jnp.float32
TOK, WIDTH, EXPERTS, CAP, HID = 128, 4096, 16, 20, 128
HALF = WIDTH // 2
ROWS = 2 * EXPERTS * CAP
STEPS = 4
COLS = HALF // STEPS
BLOCKS = WIDTH // 128


def half_of_row(shape, axis):
    row = lax.broadcasted_iota(jnp.int32, shape, axis)
    group = (row * 1639) >> 16
    rest = row - group * (2 * CAP)
    upper = rest >= CAP
    return upper, group * CAP + jnp.where(upper, rest - CAP, rest)


def targets(ids):
    expert = lax.broadcasted_iota(jnp.int32, (EXPERTS, TOK), 0)
    first = (jnp.broadcast_to(ids[0:1, :], (EXPERTS, TOK)) == expert).astype(F32)
    second = (jnp.broadcast_to(ids[1:2, :], (EXPERTS, TOK)) == expert).astype(F32)
    earlier = lax.broadcasted_iota(jnp.int32, (TOK, TOK), 0) < lax.broadcasted_iota(
        jnp.int32, (TOK, TOK), 1
    )
    before = jnp.dot(
        (first + second).astype(BF16),
        earlier.astype(F32).astype(BF16),
        preferred_element_type=F32,
    )
    rank0 = jnp.sum(first * before, 0, keepdims=True).astype(jnp.int32)
    rank1 = jnp.sum(second * before, 0, keepdims=True).astype(jnp.int32)
    return ids[0:1, :] * CAP + rank0, ids[1:2, :] * CAP + rank1


def hits(ids):
    target0, target1 = targets(ids)
    upper, slot = half_of_row((ROWS, TOK), 0)
    hit0 = slot == jnp.broadcast_to(target0, (ROWS, TOK))
    hit1 = slot == jnp.broadcast_to(target1, (ROWS, TOK))
    return hit0, hit1, upper


def placement(hit0, hit1, upper):
    hit = jnp.where(hit0 | hit1, 1.0, 0.0)
    return jnp.concatenate([jnp.where(upper, 0.0, hit), jnp.where(upper, hit, 0.0)], 1)


def place_tokens_kernel(ids_ref, low_ref, high_ref, out_ref, place):
    @pl.when(pl.program_id(0) == 0)
    def _():
        place[...] = placement(*hits(ids_ref[...])).astype(BF16)

    both = jnp.concatenate([low_ref[...], high_ref[...]], 0)
    out_ref[...] = jnp.dot(place[...], both, preferred_element_type=F32).astype(BF16)


def place_grads_kernel(ids_ref, gates_ref, low_ref, high_ref, out_ref, back_ref, place, gate):
    @pl.when(pl.program_id(0) == 0)
    def _():
        hit0, hit1, upper = hits(ids_ref[...])
        where_to = placement(hit0, hit1, upper)
        place[...] = where_to.astype(BF16)
        back_ref[...] = where_to.T.astype(BF16)
        gates = gates_ref[...]
        weight = jnp.where(hit0, jnp.broadcast_to(gates[0:1, :], (ROWS, TOK)), 0.0) + jnp.where(
            hit1, jnp.broadcast_to(gates[1:2, :], (ROWS, TOK)), 0.0
        )
        gate[...] = jnp.broadcast_to(jnp.sum(weight, 1, keepdims=True), (ROWS, 128))

    both = jnp.concatenate([low_ref[...], high_ref[...]], 0)
    picked = jnp.dot(place[...], both, preferred_element_type=F32)
    scale = gate[...]
    for i in range(COLS // 128):
        out_ref[:, i * 128 : i * 128 + 128] = (picked[:, i * 128 : i * 128 + 128] * scale).astype(
            BF16
        )


def join_halves(acc, width):
    upper, _ = half_of_row((ROWS, width), 0)
    own = jnp.where(upper, acc[:, width:], acc[:, :width])
    other = jnp.where(upper, pltpu.roll(own, CAP, 0), pltpu.roll(own, ROWS - CAP, 0))
    return own + other


def gate_up_kernel(x_ref, w_low_ref, w_high_ref, out_ref, acc):
    k = pl.program_id(0)

    @pl.when(k == 0)
    def _():
        acc[...] = jnp.zeros_like(acc)

    x = x_ref[...]
    acc[:, : 2 * HID] += jnp.dot(x, w_low_ref[:, : 2 * HID], preferred_element_type=F32)
    acc[:, 2 * HID :] += jnp.dot(x, w_high_ref[:, : 2 * HID], preferred_element_type=F32)

    @pl.when(k == STEPS - 1)
    def _():
        out_ref[...] = join_halves(acc[...], 2 * HID)


def hidden_kernel(dy_ref, w_low_ref, w_high_ref, gu_ref, both_ref, turned_ref, acc):
    k = pl.program_id(0)

    @pl.when(k == 0)
    def _():
        acc[...] = jnp.zeros_like(acc)

    weights = jnp.concatenate([w_low_ref[...], w_high_ref[...]], 1)
    acc[...] += jnp.dot(dy_ref[...], weights, preferred_element_type=F32)

    @pl.when(k == STEPS - 1)
    def _():
        hid_grad = join_halves(acc[...], HID)
        gate_pre = gu_ref[:, :HID]
        up_pre = gu_ref[:, HID:]
        sigmoid_g = jax.nn.sigmoid(gate_pre)
        silu_val = gate_pre * sigmoid_g
        silu_slope = sigmoid_g * (1.0 + gate_pre * (1.0 - sigmoid_g))
        gate_grad = hid_grad * up_pre * silu_slope
        up_grad = hid_grad * silu_val
        hidden = silu_val * up_pre
        both_ref[:, :HID] = gate_grad.astype(BF16)
        both_ref[:, HID:] = up_grad.astype(BF16)
        upper, _ = half_of_row((HID, ROWS), 1)
        for i, value in enumerate((gate_grad, up_grad, hidden)):
            turned = value.T
            turned_ref[i * HID : (i + 1) * HID, :] = jnp.where(upper, 0.0, turned).astype(BF16)
            turned_ref[(i + 3) * HID : (i + 4) * HID, :] = jnp.where(upper, turned, 0.0).astype(
                BF16
            )


def weight_grad_kernel(info_ref, turned_ref, x_ref, dy_ref, mine_ref, other_ref):
    step = pl.program_id(0)
    core = info_ref[0]
    x = x_ref[...]
    dy = dy_ref[...]
    for h in range(2):
        base = 3 * HID * h
        proj = jnp.dot(turned_ref[base : base + 2 * HID, :], x, preferred_element_type=F32)
        down = jnp.dot(
            turned_ref[base + 2 * HID : base + 3 * HID, :], dy, preferred_element_type=F32
        )
        for i in range(COLS // 128):
            block = step * (COLS // 128) + i + h * (BLOCKS // 2)
            keep = info_ref[1 + block].astype(F32)
            place = step * (COLS // 256) + i // 2 + h * (BLOCKS // 4)
            top = (proj[:, i * 128 : i * 128 + 128] * keep).astype(BF16)
            bottom = (down[:, i * 128 : i * 128 + 128] * keep).astype(BF16)

            def put(ref):
                ref[place, : 2 * HID, :] = top
                ref[place, 2 * HID :, :] = bottom

            pl.when(core == i % 2)(functools.partial(put, mine_ref))
            pl.when(core != i % 2)(functools.partial(put, other_ref))


def slot_grad_kernel(both_ref, w_low_ref, w_high_ref, out_ref):
    both = both_ref[...]
    upper, _ = half_of_row((ROWS, 2 * HID), 0)
    zero = jnp.zeros_like(both)
    dims = (((1,), (1,)), ((), ()))
    low = lax.dot_general(
        jnp.where(upper, zero, both), w_low_ref[:, : 2 * HID], dims, preferred_element_type=F32
    )
    high = lax.dot_general(
        jnp.where(upper, both, zero), w_high_ref[:, : 2 * HID], dims, preferred_element_type=F32
    )
    out_ref[...] = (low + high).astype(BF16)


def combine_kernel(back_ref, slots_ref, out_ref):
    step = pl.program_id(0)
    total = jnp.dot(back_ref[...], slots_ref[...], preferred_element_type=F32).astype(BF16)
    at = pl.multiple_of(step * COLS, COLS)
    out_ref[:, pl.ds(at, COLS)] = total[:TOK, :]
    out_ref[:, pl.ds(pl.multiple_of(at + HALF, COLS), COLS)] = total[TOK:, :]


def whole(shape):
    return pl.BlockSpec(shape, lambda i: (0,) * len(shape))


def columns(rows, shift=0):
    return pl.BlockSpec((rows, COLS), lambda i: (0, i + shift))


def weight_rows(width, shift=0, column=0):
    return pl.BlockSpec((COLS, width), lambda i: (i + shift, column))


def call(kernel, ins, outs, shapes, flops, nbytes, scratch=()):
    return pl.pallas_call(
        kernel,
        grid=(STEPS,),
        in_specs=ins,
        out_specs=outs,
        out_shape=shapes,
        scratch_shapes=list(scratch),
        compiler_params=pltpu.CompilerParams(dimension_semantics=("arbitrary",)),
        cost_estimate=pl.CostEstimate(flops=flops, bytes_accessed=nbytes, transcendentals=0),
    )


def sds(shape, dtype):
    return jax.ShapeDtypeStruct(shape, dtype)


def exchange(rows):
    return lax.all_to_all(
        rows.reshape(EXPERTS, 2 * CAP, HALF), "exp", split_axis=0, concat_axis=0, tiled=True
    ).reshape(ROWS, HALF)


def per_device(tokens, grad_out, gates, expert_ids, w_all, touched):
    rep = lax.axis_index("rep")
    reps = lax.axis_size("rep")
    ids = expert_ids.T
    mbytes = 1 << 20
    send_x = call(
        place_tokens_kernel,
        [whole((2, TOK)), columns(TOK), columns(TOK, STEPS)],
        columns(ROWS),
        sds((ROWS, HALF), BF16),
        2 * ROWS * 256 * HALF,
        4 * mbytes,
        [pltpu.VMEM((ROWS, 2 * TOK), BF16)],
    )(ids, tokens, tokens)
    slot_x = exchange(send_x)
    send_dy, back = call(
        place_grads_kernel,
        [whole((2, TOK)), whole((2, TOK)), columns(TOK), columns(TOK, STEPS)],
        [columns(ROWS), whole((2 * TOK, ROWS))],
        [sds((ROWS, HALF), BF16), sds((2 * TOK, ROWS), BF16)],
        2 * ROWS * 256 * HALF,
        4 * mbytes,
        [pltpu.VMEM((ROWS, 2 * TOK), BF16), pltpu.VMEM((ROWS, 128), F32)],
    )(ids, gates.T, grad_out, grad_out)
    slot_dy = exchange(send_dy)
    w_whole = lax.all_gather(w_all[0], "rep", axis=0, tiled=True)
    gate_up = call(
        gate_up_kernel,
        [columns(ROWS), weight_rows(3 * HID), weight_rows(3 * HID, STEPS)],
        whole((ROWS, 2 * HID)),
        sds((ROWS, 2 * HID), F32),
        2 * ROWS * HALF * 4 * HID,
        6 * mbytes,
        [pltpu.VMEM((ROWS, 4 * HID), F32)],
    )(slot_x, w_whole, w_whole)
    both_grad, turned = call(
        hidden_kernel,
        [
            columns(ROWS),
            weight_rows(HID, 0, 2),
            weight_rows(HID, STEPS, 2),
            whole((ROWS, 2 * HID)),
        ],
        [whole((ROWS, 2 * HID)), whole((6 * HID, ROWS))],
        [sds((ROWS, 2 * HID), BF16), sds((6 * HID, ROWS), BF16)],
        2 * ROWS * HALF * 2 * HID,
        4 * mbytes,
        [pltpu.VMEM((ROWS, 2 * HID), F32)],
    )(slot_dy, w_whole, w_whole, gate_up)
    info = jnp.concatenate([jnp.reshape(rep % 2, (1,)), touched.reshape(-1)])
    share = (BLOCKS // 2, 3 * HID, 128)
    mine, other = call(
        weight_grad_kernel,
        [
            pl.BlockSpec(memory_space=pltpu.SMEM),
            whole((6 * HID, ROWS)),
            columns(ROWS),
            columns(ROWS),
        ],
        [whole(share), whole(share)],
        [sds(share, BF16), sds(share, BF16)],
        2 * ROWS * HALF * 6 * HID,
        8 * mbytes,
    )(info, turned, slot_x, slot_dy)
    swap = [(i, i ^ 1) for i in range(reps)]
    received = lax.ppermute(other, "rep", swap)
    paired = (mine.astype(F32) + received.astype(F32)).astype(BF16)
    owned = lax.psum_scatter(
        paired,
        "rep",
        scatter_dimension=0,
        axis_index_groups=[list(range(c, reps, 2)) for c in range(2)],
        tiled=True,
    )
    slot_grad = call(
        slot_grad_kernel,
        [whole((ROWS, 2 * HID)), weight_rows(3 * HID), weight_rows(3 * HID, STEPS)],
        columns(ROWS),
        sds((ROWS, HALF), BF16),
        2 * ROWS * HALF * 4 * HID,
        6 * mbytes,
    )(both_grad, w_whole, w_whole)
    returned = exchange(slot_grad)
    token_grad = call(
        combine_kernel,
        [whole((2 * TOK, ROWS)), columns(ROWS)],
        whole((TOK, WIDTH)),
        sds((TOK, WIDTH), BF16),
        2 * ROWS * 256 * HALF,
        4 * mbytes,
    )(back, returned)
    weight_grad = jnp.swapaxes(owned, 1, 2).astype(F32)
    return (token_grad, weight_grad)


def solution(mesh):
    in_specs = (
        P(("rep", "exp"), None),
        P(("rep", "exp"), None),
        P(("rep", "exp"), None),
        P(("rep", "exp"), None),
        P("exp", "rep", None),
        P("rep", "exp", None),
    )
    out_specs = (P(("rep", "exp"), None), P("exp", "rep", None))
    return jax.shard_map(
        per_device, mesh=mesh, in_specs=in_specs, out_specs=out_specs, check_vma=False
    )
```

```python
import functools

import jax
import jax.numpy as jnp
from jax import lax
from jax.experimental import pallas as pl
from jax.experimental.pallas import tpu as pltpu
from jax.sharding import PartitionSpec as P

BF16 = jnp.bfloat16
F32 = jnp.float32
TOK, WIDTH, EXPERTS, CAP, HID = 128, 4096, 16, 20, 128
HALF = WIDTH // 2
ROWS = 2 * EXPERTS * CAP
STEPS = 4
COLS = HALF // STEPS
BLOCKS = WIDTH // 128


def half_of_row(shape, axis):
    row = lax.broadcasted_iota(jnp.int32, shape, axis)
    group = (row * 1639) >> 16
    rest = row - group * (2 * CAP)
    upper = rest >= CAP
    return upper, group * CAP + jnp.where(upper, rest - CAP, rest)


def targets(ids):
    expert = lax.broadcasted_iota(jnp.int32, (EXPERTS, TOK), 0)
    first = (jnp.broadcast_to(ids[0:1, :], (EXPERTS, TOK)) == expert).astype(F32)
    second = (jnp.broadcast_to(ids[1:2, :], (EXPERTS, TOK)) == expert).astype(F32)
    earlier = lax.broadcasted_iota(jnp.int32, (TOK, TOK), 0) < lax.broadcasted_iota(
        jnp.int32, (TOK, TOK), 1
    )
    before = jnp.dot(
        (first + second).astype(BF16),
        earlier.astype(F32).astype(BF16),
        preferred_element_type=F32,
    )
    rank0 = jnp.sum(first * before, 0, keepdims=True).astype(jnp.int32)
    rank1 = jnp.sum(second * before, 0, keepdims=True).astype(jnp.int32)
    return ids[0:1, :] * CAP + rank0, ids[1:2, :] * CAP + rank1


def hits(ids):
    target0, target1 = targets(ids)
    upper, slot = half_of_row((ROWS, TOK), 0)
    hit0 = slot == jnp.broadcast_to(target0, (ROWS, TOK))
    hit1 = slot == jnp.broadcast_to(target1, (ROWS, TOK))
    return hit0, hit1, upper


def placement(hit0, hit1, upper):
    hit = jnp.where(hit0 | hit1, 1.0, 0.0)
    return jnp.concatenate([jnp.where(upper, 0.0, hit), jnp.where(upper, hit, 0.0)], 1)


def place_tokens_kernel(ids_ref, low_ref, high_ref, out_ref, place):
    @pl.when(pl.program_id(0) == 0)
    def _():
        place[...] = placement(*hits(ids_ref[...])).astype(BF16)

    both = jnp.concatenate([low_ref[...], high_ref[...]], 0)
    out_ref[...] = jnp.dot(place[...], both, preferred_element_type=F32).astype(BF16)


def place_grads_kernel(ids_ref, gates_ref, low_ref, high_ref, out_ref, back_ref, place, gate):
    @pl.when(pl.program_id(0) == 0)
    def _():
        hit0, hit1, upper = hits(ids_ref[...])
        where_to = placement(hit0, hit1, upper)
        place[...] = where_to.astype(BF16)
        back_ref[...] = where_to.T.astype(BF16)
        gates = gates_ref[...]
        weight = jnp.where(hit0, jnp.broadcast_to(gates[0:1, :], (ROWS, TOK)), 0.0) + jnp.where(
            hit1, jnp.broadcast_to(gates[1:2, :], (ROWS, TOK)), 0.0
        )
        gate[...] = jnp.broadcast_to(jnp.sum(weight, 1, keepdims=True), (ROWS, 128))

    both = jnp.concatenate([low_ref[...], high_ref[...]], 0)
    picked = jnp.dot(place[...], both, preferred_element_type=F32)
    scale = gate[...]
    for i in range(COLS // 128):
        out_ref[:, i * 128 : i * 128 + 128] = (picked[:, i * 128 : i * 128 + 128] * scale).astype(
            BF16
        )


def join_halves(acc, width):
    upper, _ = half_of_row((ROWS, width), 0)
    own = jnp.where(upper, acc[:, width:], acc[:, :width])
    other = jnp.where(upper, pltpu.roll(own, CAP, 0), pltpu.roll(own, ROWS - CAP, 0))
    return own + other


def stack_rows(refs, start, stop):
    return jnp.concatenate([ref[0, :, start:stop] for ref in refs], 0)


def gate_up_kernel(table_ref, x_ref, *refs):
    del table_ref
    w_refs, (out_ref, acc) = refs[:8], refs[8:]
    k = pl.program_id(0)

    @pl.when(k == 0)
    def _():
        acc[...] = jnp.zeros_like(acc)

    x = x_ref[...]
    for h in range(2):
        weights = stack_rows(w_refs[4 * h : 4 * h + 4], 0, 2 * HID)
        acc[:, 2 * HID * h : 2 * HID * (h + 1)] += jnp.dot(
            x, weights, preferred_element_type=F32
        )

    @pl.when(k == STEPS - 1)
    def _():
        out_ref[...] = join_halves(acc[...], 2 * HID)


def hidden_kernel(table_ref, dy_ref, *refs):
    del table_ref
    w_refs, (gu_ref, both_ref, turned_ref, acc) = refs[:8], refs[8:]
    k = pl.program_id(0)

    @pl.when(k == 0)
    def _():
        acc[...] = jnp.zeros_like(acc)

    weights = jnp.concatenate(
        [stack_rows(w_refs[:4], 0, HID), stack_rows(w_refs[4:], 0, HID)], 1
    )
    acc[...] += jnp.dot(dy_ref[...], weights, preferred_element_type=F32)

    @pl.when(k == STEPS - 1)
    def _():
        hid_grad = join_halves(acc[...], HID)
        gate_pre = gu_ref[:, :HID]
        up_pre = gu_ref[:, HID:]
        sigmoid_g = jax.nn.sigmoid(gate_pre)
        silu_val = gate_pre * sigmoid_g
        silu_slope = sigmoid_g * (1.0 + gate_pre * (1.0 - sigmoid_g))
        gate_grad = hid_grad * up_pre * silu_slope
        up_grad = hid_grad * silu_val
        hidden = silu_val * up_pre
        both_ref[:, :HID] = gate_grad.astype(BF16)
        both_ref[:, HID:] = up_grad.astype(BF16)
        upper, _ = half_of_row((HID, ROWS), 1)
        for i, value in enumerate((gate_grad, up_grad, hidden)):
            turned = value.T
            turned_ref[i * HID : (i + 1) * HID, :] = jnp.where(upper, 0.0, turned).astype(BF16)
            turned_ref[(i + 3) * HID : (i + 4) * HID, :] = jnp.where(upper, turned, 0.0).astype(
                BF16
            )


def weight_grad_kernel(
    info_ref, turned_ref, x_ref, dy_ref, odd_ref, even_ref, far_ref, give_odd_ref, give_rest_ref
):
    step = pl.program_id(0)
    x = x_ref[...]
    dy = dy_ref[...]
    spans = ((odd_ref, 0, 8), (even_ref, 8, 16), (far_ref, 16, 17), (give_odd_ref, 17, 25))
    spans += ((give_rest_ref, 25, 32),)
    for h in range(2):
        base = 3 * HID * h
        proj = jnp.dot(turned_ref[base : base + 2 * HID, :], x, preferred_element_type=F32)
        down = jnp.dot(
            turned_ref[base + 2 * HID : base + 3 * HID, :], dy, preferred_element_type=F32
        )
        for i in range(COLS // 128):
            block = step * (COLS // 128) + i + h * (BLOCKS // 2)
            keep = info_ref[block].astype(F32)
            place = info_ref[BLOCKS + block]
            top = (proj[:, i * 128 : i * 128 + 128] * keep).astype(BF16)
            bottom = (down[:, i * 128 : i * 128 + 128] * keep).astype(BF16)

            def put(ref, first):
                ref[place - first, : 2 * HID, :] = top
                ref[place - first, 2 * HID :, :] = bottom

            for ref, first, last in spans:
                pl.when((place >= first) & (place < last))(functools.partial(put, ref, first))


def slot_grad_kernel(table_ref, both_ref, *refs):
    del table_ref
    w_refs, out_ref = refs[:8], refs[8]
    both = both_ref[...]
    upper, _ = half_of_row((ROWS, 2 * HID), 0)
    zero = jnp.zeros_like(both)
    total = None
    for h in range(2):
        own = jnp.where(upper, both, zero) if h else jnp.where(upper, zero, both)
        part = lax.dot_general(
            own,
            stack_rows(w_refs[4 * h : 4 * h + 4], 0, 2 * HID),
            (((1,), (1,)), ((), ())),
            preferred_element_type=F32,
        )
        total = part if total is None else total + part
    out_ref[...] = total.astype(BF16)


def combine_kernel(back_ref, slots_ref, out_ref):
    step = pl.program_id(0)
    total = jnp.dot(back_ref[...], slots_ref[...], preferred_element_type=F32).astype(BF16)
    at = pl.multiple_of(step * COLS, COLS)
    out_ref[:, pl.ds(at, COLS)] = total[:TOK, :]
    out_ref[:, pl.ds(pl.multiple_of(at + HALF, COLS), COLS)] = total[TOK:, :]


def whole(shape):
    return pl.BlockSpec(shape, lambda i, *_: (0,) * len(shape))


def columns(rows, shift=0):
    return pl.BlockSpec((rows, COLS), lambda i, *_: (0, i + shift))


def weight_blocks(width, column=0):
    return [
        pl.BlockSpec(
            (1, 128, width),
            lambda i, table, first=BLOCKS // 2 * h + j: (table[4 * i + first], 0, column),
        )
        for h in range(2)
        for j in range(4)
    ]


def call(kernel, ins, outs, shapes, flops, nbytes, scratch=(), prefetch=0):
    return pl.pallas_call(
        kernel,
        grid_spec=pltpu.PrefetchScalarGridSpec(
            num_scalar_prefetch=prefetch,
            grid=(STEPS,),
            in_specs=ins,
            out_specs=outs,
            scratch_shapes=list(scratch),
        ),
        out_shape=shapes,
        compiler_params=pltpu.CompilerParams(dimension_semantics=("arbitrary",)),
        cost_estimate=pl.CostEstimate(flops=flops, bytes_accessed=nbytes, transcendentals=0),
    )


def sds(shape, dtype):
    return jax.ShapeDtypeStruct(shape, dtype)


def exchange(rows):
    return lax.all_to_all(
        rows.reshape(EXPERTS, 2 * CAP, HALF), "exp", split_axis=0, concat_axis=0, tiled=True
    ).reshape(ROWS, HALF)


def hop(value, distance):
    reps = lax.axis_size("rep")
    turn = [
        (i, (i + 2 * distance) % reps if i % 2 == 0 else (i - 2 * distance) % reps)
        for i in range(reps)
    ]
    return lax.ppermute(value, "rep", turn)


def swap(value):
    return lax.ppermute(value, "rep", [(i, i ^ 1) for i in range(lax.axis_size("rep"))])


def places(rep, sign):
    block = jnp.arange(BLOCKS, dtype=jnp.int32)
    core = rep & 1
    kind = block & 1
    ahead = (sign * ((block >> 1) - (rep >> 1))) & 15
    carrier = jnp.where(ahead == 8, kind, (ahead > 8).astype(jnp.int32))
    distance = jnp.where(ahead > 8, 16 - ahead, ahead)
    carrier = jnp.where(ahead == 0, core, carrier)
    index = (distance & 2) + ((distance >> 2) & 1)
    pair = 2 * index + (kind != carrier).astype(jnp.int32)
    return distance == 8, (distance & 1) == 1, pair, carrier == core


def gathered_places(rep):
    far, odd, pair, local = places(rep, -1)
    at = jnp.where(far, 16, jnp.where(odd, 8, 0) + pair)
    return jnp.where(local, at, at + 15)


def scattered_places(rep):
    far, odd, pair, local = places(rep, 1)
    kept = jnp.where(far, 16, jnp.where(odd, 0, 8) + pair)
    given = jnp.where(far, 31, jnp.where(odd, 17, 23) + pair)
    return jnp.where(local, kept, given)


def gather_weights(own):
    near = jnp.stack([own, swap(own)])
    far = hop(own[None], 8)
    fourth = hop(near, 4)
    fours = jnp.concatenate([near, fourth])
    second = hop(fours, 2)
    eights = jnp.concatenate([fours, second])
    first = hop(eights, 1)
    rest = jnp.concatenate([fourth, second])
    return jnp.concatenate(
        [eights, first, far, swap(rest), swap(first), swap(far)]
    )


def scatter_sum(odd, even, far, give_odd, give_rest):
    def add(*parts):
        return functools.reduce(jnp.add, [part.astype(F32) for part in parts])

    odd = add(odd, swap(give_odd)).astype(BF16)
    got = swap(give_rest)
    one = hop(odd, 1)
    far = hop(add(far, got[6:]).astype(BF16), 8)
    two = hop(add(even[4:], got[2:6], one[4:]).astype(BF16), 2)
    four = hop(add(even[2:4], got[:2], one[2:4], two[2:]).astype(BF16), 4)
    here = add(even[:2], one[:2], two[:2], four)
    return here[:1] + add(far, swap(here[1:].astype(BF16)))


def per_device(tokens, grad_out, gates, expert_ids, w_all, touched):
    rep = lax.axis_index("rep")
    ids = expert_ids.T
    mbytes = 1 << 20
    send_x = call(
        place_tokens_kernel,
        [whole((2, TOK)), columns(TOK), columns(TOK, STEPS)],
        columns(ROWS),
        sds((ROWS, HALF), BF16),
        2 * ROWS * 256 * HALF,
        4 * mbytes,
        [pltpu.VMEM((ROWS, 2 * TOK), BF16)],
    )(ids, tokens, tokens)
    slot_x = exchange(send_x)
    send_dy, back = call(
        place_grads_kernel,
        [whole((2, TOK)), whole((2, TOK)), columns(TOK), columns(TOK, STEPS)],
        [columns(ROWS), whole((2 * TOK, ROWS))],
        [sds((ROWS, HALF), BF16), sds((2 * TOK, ROWS), BF16)],
        2 * ROWS * 256 * HALF,
        4 * mbytes,
        [pltpu.VMEM((ROWS, 2 * TOK), BF16), pltpu.VMEM((ROWS, 128), F32)],
    )(ids, gates.T, grad_out, grad_out)
    slot_dy = exchange(send_dy)
    w_whole = gather_weights(w_all[0])
    table = gathered_places(rep)
    gate_up = call(
        gate_up_kernel,
        [columns(ROWS)] + weight_blocks(3 * HID),
        whole((ROWS, 2 * HID)),
        sds((ROWS, 2 * HID), F32),
        2 * ROWS * HALF * 4 * HID,
        6 * mbytes,
        [pltpu.VMEM((ROWS, 4 * HID), F32)],
        1,
    )(table, slot_x, *[w_whole] * 8)
    both_grad, turned = call(
        hidden_kernel,
        [columns(ROWS)] + weight_blocks(HID, 2) + [whole((ROWS, 2 * HID))],
        [whole((ROWS, 2 * HID)), whole((6 * HID, ROWS))],
        [sds((ROWS, 2 * HID), BF16), sds((6 * HID, ROWS), BF16)],
        2 * ROWS * HALF * 2 * HID,
        4 * mbytes,
        [pltpu.VMEM((ROWS, 2 * HID), F32)],
        1,
    )(table, slot_dy, *[w_whole] * 8, gate_up)
    info = jnp.concatenate([touched.reshape(-1), scattered_places(rep)])
    shares = [(n, 3 * HID, 128) for n in (8, 8, 1, 8, 7)]
    pieces = call(
        weight_grad_kernel,
        [
            pl.BlockSpec(memory_space=pltpu.SMEM),
            whole((6 * HID, ROWS)),
            columns(ROWS),
            columns(ROWS),
        ],
        [whole(share) for share in shares],
        [sds(share, BF16) for share in shares],
        2 * ROWS * HALF * 6 * HID,
        8 * mbytes,
    )(info, turned, slot_x, slot_dy)
    owned = scatter_sum(*pieces)
    slot_grad = call(
        slot_grad_kernel,
        [whole((ROWS, 2 * HID))] + weight_blocks(3 * HID),
        columns(ROWS),
        sds((ROWS, HALF), BF16),
        2 * ROWS * HALF * 4 * HID,
        6 * mbytes,
        (),
        1,
    )(table, both_grad, *[w_whole] * 8)
    returned = exchange(slot_grad)
    token_grad = call(
        combine_kernel,
        [whole((2 * TOK, ROWS)), columns(ROWS)],
        whole((TOK, WIDTH)),
        sds((TOK, WIDTH), BF16),
        2 * ROWS * 256 * HALF,
        4 * mbytes,
    )(back, returned)
    return (token_grad, jnp.swapaxes(owned, 1, 2))


def solution(mesh):
    in_specs = (
        P(("rep", "exp"), None),
        P(("rep", "exp"), None),
        P(("rep", "exp"), None),
        P(("rep", "exp"), None),
        P("exp", "rep", None),
        P("rep", "exp", None),
    )
    out_specs = (P(("rep", "exp"), None), P("exp", "rep", None))
    return jax.shard_map(
        per_device, mesh=mesh, in_specs=in_specs, out_specs=out_specs, check_vma=False
    )
```

```python
import functools

import jax
import jax.numpy as jnp
from jax import lax
from jax.experimental import pallas as pl
from jax.experimental.pallas import tpu as pltpu
from jax.sharding import PartitionSpec as P

BF16 = jnp.bfloat16
F32 = jnp.float32
TOK, WIDTH, EXPERTS, CAP, HID = 128, 4096, 16, 20, 128
HALF = WIDTH // 2
ROWS = 2 * EXPERTS * CAP
STEPS = 4
COLS = HALF // STEPS
BLOCKS = WIDTH // 128


def half_of_row(shape, axis):
    row = lax.broadcasted_iota(jnp.int32, shape, axis)
    group = (row * 1639) >> 16
    rest = row - group * (2 * CAP)
    upper = rest >= CAP
    return upper, group * CAP + jnp.where(upper, rest - CAP, rest)


def targets(ids):
    expert = lax.broadcasted_iota(jnp.int32, (EXPERTS, TOK), 0)
    first = (jnp.broadcast_to(ids[0:1, :], (EXPERTS, TOK)) == expert).astype(F32)
    second = (jnp.broadcast_to(ids[1:2, :], (EXPERTS, TOK)) == expert).astype(F32)
    earlier = lax.broadcasted_iota(jnp.int32, (TOK, TOK), 0) < lax.broadcasted_iota(
        jnp.int32, (TOK, TOK), 1
    )
    before = jnp.dot(
        (first + second).astype(BF16),
        earlier.astype(F32).astype(BF16),
        preferred_element_type=F32,
    )
    rank0 = jnp.sum(first * before, 0, keepdims=True).astype(jnp.int32)
    rank1 = jnp.sum(second * before, 0, keepdims=True).astype(jnp.int32)
    return ids[0:1, :] * CAP + rank0, ids[1:2, :] * CAP + rank1


def hits(ids):
    target0, target1 = targets(ids)
    upper, slot = half_of_row((ROWS, TOK), 0)
    hit0 = slot == jnp.broadcast_to(target0, (ROWS, TOK))
    hit1 = slot == jnp.broadcast_to(target1, (ROWS, TOK))
    return hit0, hit1, upper


def placement(hit0, hit1, upper):
    hit = jnp.where(hit0 | hit1, 1.0, 0.0)
    return jnp.concatenate([jnp.where(upper, 0.0, hit), jnp.where(upper, hit, 0.0)], 1)


def place_tokens_kernel(ids_ref, low_ref, high_ref, out_ref, place):
    @pl.when(pl.program_id(0) == 0)
    def _():
        place[...] = placement(*hits(ids_ref[...])).astype(BF16)

    both = jnp.concatenate([low_ref[...], high_ref[...]], 0)
    out_ref[...] = jnp.dot(place[...], both, preferred_element_type=F32).astype(BF16)


def place_grads_kernel(ids_ref, gates_ref, low_ref, high_ref, out_ref, back_ref, place, gate):
    @pl.when(pl.program_id(0) == 0)
    def _():
        hit0, hit1, upper = hits(ids_ref[...])
        where_to = placement(hit0, hit1, upper)
        place[...] = where_to.astype(BF16)
        back_ref[...] = where_to.T.astype(BF16)
        gates = gates_ref[...]
        weight = jnp.where(hit0, jnp.broadcast_to(gates[0:1, :], (ROWS, TOK)), 0.0) + jnp.where(
            hit1, jnp.broadcast_to(gates[1:2, :], (ROWS, TOK)), 0.0
        )
        gate[...] = jnp.broadcast_to(jnp.sum(weight, 1, keepdims=True), (ROWS, 128))

    both = jnp.concatenate([low_ref[...], high_ref[...]], 0)
    picked = jnp.dot(place[...], both, preferred_element_type=F32)
    scale = gate[...]
    for i in range(COLS // 128):
        out_ref[:, i * 128 : i * 128 + 128] = (picked[:, i * 128 : i * 128 + 128] * scale).astype(
            BF16
        )


def join_halves(acc, width):
    upper, _ = half_of_row((ROWS, width), 0)
    own = jnp.where(upper, acc[:, width:], acc[:, :width])
    other = jnp.where(upper, pltpu.roll(own, CAP, 0), pltpu.roll(own, ROWS - CAP, 0))
    return own + other


def stack_rows(refs, start, stop):
    return jnp.concatenate([ref[0, :, start:stop] for ref in refs], 0)


def gate_up_kernel(table_ref, x_ref, *refs):
    del table_ref
    w_refs, (out_ref, acc) = refs[:8], refs[8:]
    k = pl.program_id(0)

    @pl.when(k == 0)
    def _():
        acc[...] = jnp.zeros_like(acc)

    x = x_ref[...]
    for h in range(2):
        weights = stack_rows(w_refs[4 * h : 4 * h + 4], 0, 2 * HID)
        acc[:, 2 * HID * h : 2 * HID * (h + 1)] += jnp.dot(
            x, weights, preferred_element_type=F32
        )

    @pl.when(k == STEPS - 1)
    def _():
        out_ref[...] = join_halves(acc[...], 2 * HID)


def hidden_kernel(table_ref, dy_ref, *refs):
    del table_ref
    w_refs, (gu_ref, both_ref, turned_ref, acc) = refs[:8], refs[8:]
    k = pl.program_id(0)

    @pl.when(k == 0)
    def _():
        acc[...] = jnp.zeros_like(acc)

    weights = jnp.concatenate(
        [stack_rows(w_refs[:4], 0, HID), stack_rows(w_refs[4:], 0, HID)], 1
    )
    acc[...] += jnp.dot(dy_ref[...], weights, preferred_element_type=F32)

    @pl.when(k == STEPS - 1)
    def _():
        hid_grad = join_halves(acc[...], HID)
        gate_pre = gu_ref[:, :HID]
        up_pre = gu_ref[:, HID:]
        sigmoid_g = jax.nn.sigmoid(gate_pre)
        silu_val = gate_pre * sigmoid_g
        silu_slope = sigmoid_g * (1.0 + gate_pre * (1.0 - sigmoid_g))
        gate_grad = hid_grad * up_pre * silu_slope
        up_grad = hid_grad * silu_val
        hidden = silu_val * up_pre
        both_ref[:, :HID] = gate_grad.astype(BF16)
        both_ref[:, HID:] = up_grad.astype(BF16)
        upper, _ = half_of_row((HID, ROWS), 1)
        for i, value in enumerate((gate_grad, up_grad, hidden)):
            turned = value.T
            turned_ref[i * HID : (i + 1) * HID, :] = jnp.where(upper, 0.0, turned).astype(BF16)
            turned_ref[(i + 3) * HID : (i + 4) * HID, :] = jnp.where(upper, turned, 0.0).astype(
                BF16
            )


def weight_grad_kernel(
    info_ref, turned_ref, x_ref, dy_ref, even_ref, odd_ref, here_ref, give_even_ref, give_odd_ref
):
    step = pl.program_id(0)
    x = x_ref[...]
    dy = dy_ref[...]
    spans = ((even_ref, 0, 7), (odd_ref, 7, 15), (here_ref, 15, 17), (give_even_ref, 17, 24))
    spans += ((give_odd_ref, 24, 32),)
    for h in range(2):
        base = 3 * HID * h
        proj = jnp.dot(turned_ref[base : base + 2 * HID, :], x, preferred_element_type=F32)
        down = jnp.dot(
            turned_ref[base + 2 * HID : base + 3 * HID, :], dy, preferred_element_type=F32
        )
        for i in range(COLS // 128):
            block = step * (COLS // 128) + i + h * (BLOCKS // 2)
            keep = info_ref[block].astype(F32)
            place = info_ref[BLOCKS + block]
            top = (proj[:, i * 128 : i * 128 + 128] * keep).astype(BF16)
            bottom = (down[:, i * 128 : i * 128 + 128] * keep).astype(BF16)

            def put(ref, first):
                ref[place - first, : 2 * HID, :] = top
                ref[place - first, 2 * HID :, :] = bottom

            for ref, first, last in spans:
                pl.when((place >= first) & (place < last))(functools.partial(put, ref, first))


def slot_grad_kernel(table_ref, both_ref, *refs):
    del table_ref
    w_refs, out_ref = refs[:8], refs[8]
    both = both_ref[...]
    upper, _ = half_of_row((ROWS, 2 * HID), 0)
    zero = jnp.zeros_like(both)
    total = None
    for h in range(2):
        own = jnp.where(upper, both, zero) if h else jnp.where(upper, zero, both)
        part = lax.dot_general(
            own,
            stack_rows(w_refs[4 * h : 4 * h + 4], 0, 2 * HID),
            (((1,), (1,)), ((), ())),
            preferred_element_type=F32,
        )
        total = part if total is None else total + part
    out_ref[...] = total.astype(BF16)


def combine_kernel(back_ref, slots_ref, out_ref):
    step = pl.program_id(0)
    total = jnp.dot(back_ref[...], slots_ref[...], preferred_element_type=F32).astype(BF16)
    at = pl.multiple_of(step * COLS, COLS)
    out_ref[:, pl.ds(at, COLS)] = total[:TOK, :]
    out_ref[:, pl.ds(pl.multiple_of(at + HALF, COLS), COLS)] = total[TOK:, :]


def whole(shape):
    return pl.BlockSpec(shape, lambda i, *_: (0,) * len(shape))


def columns(rows, shift=0):
    return pl.BlockSpec((rows, COLS), lambda i, *_: (0, i + shift))


def weight_blocks(width, column=0):
    return [
        pl.BlockSpec(
            (1, 128, width),
            lambda i, table, first=BLOCKS // 2 * h + j: (table[4 * i + first], 0, column),
        )
        for h in range(2)
        for j in range(4)
    ]


def call(kernel, ins, outs, shapes, flops, nbytes, scratch=(), prefetch=0):
    return pl.pallas_call(
        kernel,
        grid_spec=pltpu.PrefetchScalarGridSpec(
            num_scalar_prefetch=prefetch,
            grid=(STEPS,),
            in_specs=ins,
            out_specs=outs,
            scratch_shapes=list(scratch),
        ),
        out_shape=shapes,
        compiler_params=pltpu.CompilerParams(dimension_semantics=("arbitrary",)),
        cost_estimate=pl.CostEstimate(flops=flops, bytes_accessed=nbytes, transcendentals=0),
    )


def sds(shape, dtype):
    return jax.ShapeDtypeStruct(shape, dtype)


def exchange(rows):
    return lax.all_to_all(
        rows.reshape(EXPERTS, 2 * CAP, HALF), "exp", split_axis=0, concat_axis=0, tiled=True
    ).reshape(ROWS, HALF)


def hop(value, distance):
    reps = lax.axis_size("rep")
    turn = [
        (i, (i + 2 * distance) % reps if i % 2 == 0 else (i - 2 * distance) % reps)
        for i in range(reps)
    ]
    return lax.ppermute(value, "rep", turn)


def swap(value):
    return lax.ppermute(value, "rep", [(i, i ^ 1) for i in range(lax.axis_size("rep"))])


def places(rep, sign):
    block = jnp.arange(BLOCKS, dtype=jnp.int32)
    core = rep & 1
    kind = block & 1
    ahead = (sign * ((block >> 1) - (rep >> 1))) & 15
    carrier = jnp.where(ahead == 8, kind, (ahead > 8).astype(jnp.int32))
    carrier = jnp.where(ahead == 0, core, carrier)
    distance = jnp.where(ahead > 8, 16 - ahead, ahead)
    odd = (distance & 1) == 1
    step = jnp.where(odd, distance, distance - 1)
    second = (kind != carrier).astype(jnp.int32)
    pair = 2 * ((step & 2) + ((step >> 2) & 1)) + second
    return distance == 0, odd, pair, second, carrier == core


def gathered_places(rep):
    here, odd, pair, second, local = places(rep, -1)
    at = jnp.where(here, second, jnp.where(odd, 2, 10) + pair)
    return jnp.where(local, at, at + 16)


def scattered_places(rep):
    here, odd, pair, second, local = places(rep, 1)
    at = jnp.where(here, 15 + second, jnp.where(odd, 7, 0) + pair)
    return jnp.where(local, at, at + 17)


def join_kernel(count, *refs):
    out, sems = refs[count:]
    copies, at = [], 0
    for i, piece in enumerate(refs[:count]):
        span = piece.shape[0]
        copies.append(pltpu.make_async_copy(piece, out.at[pl.ds(at, span)], sems.at[i]))
        copies[-1].start()
        at += span
    for copy in copies:
        copy.wait()


def join(pieces):
    blocks = sum(piece.shape[0] for piece in pieces)
    return pl.pallas_call(
        functools.partial(join_kernel, len(pieces)),
        in_specs=[pl.BlockSpec(memory_space=pl.ANY)] * len(pieces),
        out_specs=pl.BlockSpec(memory_space=pltpu.VMEM),
        out_shape=sds((blocks,) + pieces[0].shape[1:], pieces[0].dtype),
        scratch_shapes=[pltpu.SemaphoreType.DMA((len(pieces),))],
        cost_estimate=pl.CostEstimate(flops=0, bytes_accessed=8 << 20, transcendentals=0),
    )(*pieces)


def gather_weights(own):
    near = jnp.stack([own, swap(own)])
    one = hop(near, 1)
    five = hop(one, 4)
    three_seven = hop(jnp.concatenate([one, five]), 2)
    odd = jnp.concatenate([one, five, three_seven])
    even = hop(odd, 1)
    return join([near, odd, even, swap(odd), swap(even)])


def scatter_sum(even, odd, here, give_even, give_odd):
    def add(*parts):
        return functools.reduce(jnp.add, [part.astype(F32) for part in parts])

    one = hop(add(even, swap(give_even)).astype(BF16), 1)
    got = swap(give_odd)
    last = jnp.pad(one[4:], ((0, 1), (0, 0), (0, 0)))
    two = hop(add(odd[4:], got[4:], last).astype(BF16), 2)
    four = hop(add(odd[2:4], got[2:4], one[2:4], two[2:]).astype(BF16), 4)
    final = hop(add(odd[:2], got[:2], one[:2], two[:2], four).astype(BF16), 1)
    total = add(here, final)
    return total[:1] + swap(total[1:].astype(BF16)).astype(F32)


def per_device(tokens, grad_out, gates, expert_ids, w_all, touched):
    rep = lax.axis_index("rep")
    ids = expert_ids.T
    mbytes = 1 << 20
    send_x = call(
        place_tokens_kernel,
        [whole((2, TOK)), columns(TOK), columns(TOK, STEPS)],
        columns(ROWS),
        sds((ROWS, HALF), BF16),
        2 * ROWS * 256 * HALF,
        4 * mbytes,
        [pltpu.VMEM((ROWS, 2 * TOK), BF16)],
    )(ids, tokens, tokens)
    slot_x = exchange(send_x)
    send_dy, back = call(
        place_grads_kernel,
        [whole((2, TOK)), whole((2, TOK)), columns(TOK), columns(TOK, STEPS)],
        [columns(ROWS), whole((2 * TOK, ROWS))],
        [sds((ROWS, HALF), BF16), sds((2 * TOK, ROWS), BF16)],
        2 * ROWS * 256 * HALF,
        4 * mbytes,
        [pltpu.VMEM((ROWS, 2 * TOK), BF16), pltpu.VMEM((ROWS, 128), F32)],
    )(ids, gates.T, grad_out, grad_out)
    slot_dy = exchange(send_dy)
    w_whole = gather_weights(w_all[0])
    table = gathered_places(rep)
    gate_up = call(
        gate_up_kernel,
        [columns(ROWS)] + weight_blocks(3 * HID),
        whole((ROWS, 2 * HID)),
        sds((ROWS, 2 * HID), F32),
        2 * ROWS * HALF * 4 * HID,
        6 * mbytes,
        [pltpu.VMEM((ROWS, 4 * HID), F32)],
        1,
    )(table, slot_x, *[w_whole] * 8)
    both_grad, turned = call(
        hidden_kernel,
        [columns(ROWS)] + weight_blocks(HID, 2) + [whole((ROWS, 2 * HID))],
        [whole((ROWS, 2 * HID)), whole((6 * HID, ROWS))],
        [sds((ROWS, 2 * HID), BF16), sds((6 * HID, ROWS), BF16)],
        2 * ROWS * HALF * 2 * HID,
        4 * mbytes,
        [pltpu.VMEM((ROWS, 2 * HID), F32)],
        1,
    )(table, slot_dy, *[w_whole] * 8, gate_up)
    info = jnp.concatenate([touched.reshape(-1), scattered_places(rep)])
    shares = [(n, 3 * HID, 128) for n in (7, 8, 2, 7, 8)]
    pieces = call(
        weight_grad_kernel,
        [
            pl.BlockSpec(memory_space=pltpu.SMEM),
            whole((6 * HID, ROWS)),
            columns(ROWS),
            columns(ROWS),
        ],
        [whole(share) for share in shares],
        [sds(share, BF16) for share in shares],
        2 * ROWS * HALF * 6 * HID,
        8 * mbytes,
    )(info, turned, slot_x, slot_dy)
    owned = scatter_sum(*pieces)
    slot_grad = call(
        slot_grad_kernel,
        [whole((ROWS, 2 * HID))] + weight_blocks(3 * HID),
        columns(ROWS),
        sds((ROWS, HALF), BF16),
        2 * ROWS * HALF * 4 * HID,
        6 * mbytes,
        (),
        1,
    )(table, both_grad, *[w_whole] * 8)
    returned = exchange(slot_grad)
    token_grad = call(
        combine_kernel,
        [whole((2 * TOK, ROWS)), columns(ROWS)],
        whole((TOK, WIDTH)),
        sds((TOK, WIDTH), BF16),
        2 * ROWS * 256 * HALF,
        4 * mbytes,
    )(back, returned)
    return (token_grad, jnp.swapaxes(owned, 1, 2))


def solution(mesh):
    in_specs = (
        P(("rep", "exp"), None),
        P(("rep", "exp"), None),
        P(("rep", "exp"), None),
        P(("rep", "exp"), None),
        P("exp", "rep", None),
        P("rep", "exp", None),
    )
    out_specs = (P(("rep", "exp"), None), P("exp", "rep", None))
    return jax.shard_map(
        per_device, mesh=mesh, in_specs=in_specs, out_specs=out_specs, check_vma=False
    )
```

```python
import functools

import jax
import jax.numpy as jnp
from jax import lax
from jax.experimental import pallas as pl
from jax.experimental.pallas import tpu as pltpu
from jax.sharding import PartitionSpec as P

BF16 = jnp.bfloat16
F32 = jnp.float32
TOK, WIDTH, EXPERTS, CAP, HID = 128, 4096, 16, 20, 128
HALF = WIDTH // 2
ROWS = 2 * EXPERTS * CAP
STEPS = 4
COLS = HALF // STEPS
BLOCKS = WIDTH // 128


def half_of_row(shape, axis):
    row = lax.broadcasted_iota(jnp.int32, shape, axis)
    group = (row * 1639) >> 16
    rest = row - group * (2 * CAP)
    upper = rest >= CAP
    return upper, group * CAP + jnp.where(upper, rest - CAP, rest)


def targets(ids):
    expert = lax.broadcasted_iota(jnp.int32, (EXPERTS, TOK), 0)
    first = (jnp.broadcast_to(ids[0:1, :], (EXPERTS, TOK)) == expert).astype(F32)
    second = (jnp.broadcast_to(ids[1:2, :], (EXPERTS, TOK)) == expert).astype(F32)
    earlier = lax.broadcasted_iota(jnp.int32, (TOK, TOK), 0) < lax.broadcasted_iota(
        jnp.int32, (TOK, TOK), 1
    )
    before = jnp.dot(
        (first + second).astype(BF16),
        earlier.astype(F32).astype(BF16),
        preferred_element_type=F32,
    )
    rank0 = jnp.sum(first * before, 0, keepdims=True).astype(jnp.int32)
    rank1 = jnp.sum(second * before, 0, keepdims=True).astype(jnp.int32)
    return ids[0:1, :] * CAP + rank0, ids[1:2, :] * CAP + rank1


def hits(ids):
    target0, target1 = targets(ids)
    upper, slot = half_of_row((ROWS, TOK), 0)
    hit0 = slot == jnp.broadcast_to(target0, (ROWS, TOK))
    hit1 = slot == jnp.broadcast_to(target1, (ROWS, TOK))
    return hit0, hit1, upper


def placement(hit0, hit1, upper):
    hit = jnp.where(hit0 | hit1, 1.0, 0.0)
    return jnp.concatenate([jnp.where(upper, 0.0, hit), jnp.where(upper, hit, 0.0)], 1)


def place_kernel(
    ids_ref, gates_ref, x_low_ref, x_high_ref, dy_low_ref, dy_high_ref, out_ref, place, gate
):
    step = pl.program_id(0)

    @pl.when(step == 0)
    def _():
        place[...] = placement(*hits(ids_ref[...])).astype(BF16)

    @pl.when(step < STEPS)
    def _():
        both = jnp.concatenate([x_low_ref[...], x_high_ref[...]], 0)
        out_ref[...] = jnp.dot(place[...], both, preferred_element_type=F32).astype(BF16)

    @pl.when(step == STEPS)
    def _():
        hit0, hit1, _ = hits(ids_ref[...])
        gates = gates_ref[...]
        weight = jnp.where(hit0, jnp.broadcast_to(gates[0:1, :], (ROWS, TOK)), 0.0) + jnp.where(
            hit1, jnp.broadcast_to(gates[1:2, :], (ROWS, TOK)), 0.0
        )
        gate[...] = jnp.broadcast_to(jnp.sum(weight, 1, keepdims=True), (ROWS, 128))

    @pl.when(step >= STEPS)
    def _():
        both = jnp.concatenate([dy_low_ref[...], dy_high_ref[...]], 0)
        picked = jnp.dot(place[...], both, preferred_element_type=F32)
        scale = gate[...]
        for i in range(COLS // 128):
            part = picked[:, i * 128 : i * 128 + 128] * scale
            out_ref[:, i * 128 : i * 128 + 128] = part.astype(BF16)


def back_kernel(ids_ref, back_ref):
    back_ref[...] = placement(*hits(ids_ref[...])).T.astype(BF16)


def join_halves(acc, width):
    upper, _ = half_of_row((ROWS, width), 0)
    own = jnp.where(upper, acc[:, width:], acc[:, :width])
    other = jnp.where(upper, pltpu.roll(own, CAP, 0), pltpu.roll(own, ROWS - CAP, 0))
    return own + other


def stack_rows(refs, start, stop):
    return jnp.concatenate([ref[0, :, start:stop] for ref in refs], 0)


def column_copy(recv_ref, slots, sems, i):
    at = pl.ds(pl.multiple_of(i * COLS, COLS), COLS)
    return pltpu.make_async_copy(recv_ref.at[:, at], slots.at[:, at], sems.at[i])


def expert_kernel(table_ref, info_ref, recv_ref, *refs):
    del table_ref
    w_refs, both_ref, pieces = refs[:8], refs[8], refs[9:14]
    slots, turned_ref, gate_up, down, sems = refs[14:]
    step = pl.program_id(0)

    @pl.when(step == 0)
    def _():
        for i in range(2 * STEPS):
            column_copy(recv_ref, slots, sems, i).start()
        gate_up[...] = jnp.zeros_like(gate_up)
        down[...] = jnp.zeros_like(down)

    @pl.when(step < 2 * STEPS)
    def _():
        column_copy(recv_ref, slots, sems, step).wait()

    @pl.when(step < STEPS)
    def _():
        x = slots[:, pl.ds(pl.multiple_of(step * COLS, COLS), COLS)]
        for h in range(2):
            weights = stack_rows(w_refs[4 * h : 4 * h + 4], 0, 2 * HID)
            gate_up[:, 2 * HID * h : 2 * HID * (h + 1)] += jnp.dot(
                x, weights, preferred_element_type=F32
            )

    @pl.when((step >= STEPS) & (step < 2 * STEPS))
    def _():
        dy = slots[:, pl.ds(pl.multiple_of(step * COLS, COLS), COLS)]
        weights = jnp.concatenate(
            [stack_rows(w_refs[:4], 2 * HID, 3 * HID), stack_rows(w_refs[4:], 2 * HID, 3 * HID)],
            1,
        )
        down[...] += jnp.dot(dy, weights, preferred_element_type=F32)

    @pl.when(step == 2 * STEPS - 1)
    def _():
        joined = join_halves(gate_up[...], 2 * HID)
        hid_grad = join_halves(down[...], HID)
        gate_pre = joined[:, :HID]
        up_pre = joined[:, HID:]
        sigmoid_g = jax.nn.sigmoid(gate_pre)
        silu_val = gate_pre * sigmoid_g
        silu_slope = sigmoid_g * (1.0 + gate_pre * (1.0 - sigmoid_g))
        gate_grad = hid_grad * up_pre * silu_slope
        up_grad = hid_grad * silu_val
        hidden = silu_val * up_pre
        both_ref[:, :HID] = gate_grad.astype(BF16)
        both_ref[:, HID:] = up_grad.astype(BF16)
        upper, _ = half_of_row((HID, ROWS), 1)
        for i, value in enumerate((gate_grad, up_grad, hidden)):
            turned = value.T
            turned_ref[i * HID : (i + 1) * HID, :] = jnp.where(upper, 0.0, turned).astype(BF16)
            turned_ref[(i + 3) * HID : (i + 4) * HID, :] = jnp.where(upper, turned, 0.0).astype(
                BF16
            )

    @pl.when(step >= 2 * STEPS)
    def _():
        weight_grad(info_ref, step - 2 * STEPS, slots, turned_ref, pieces)


def weight_grad(info_ref, step, slots, turned_ref, pieces):
    at = pl.multiple_of(step * COLS, COLS)
    x = slots[:, pl.ds(at, COLS)]
    dy = slots[:, pl.ds(pl.multiple_of(at + HALF, COLS), COLS)]
    spans = tuple(zip(pieces, (0, 7, 15, 17, 24), (7, 15, 17, 24, 32)))
    for h in range(2):
        base = 3 * HID * h
        proj = jnp.dot(turned_ref[base : base + 2 * HID, :], x, preferred_element_type=F32)
        down = jnp.dot(
            turned_ref[base + 2 * HID : base + 3 * HID, :], dy, preferred_element_type=F32
        )
        for i in range(COLS // 128):
            block = step * (COLS // 128) + i + h * (BLOCKS // 2)
            keep = info_ref[block].astype(F32)
            place = info_ref[BLOCKS + block]
            top = (proj[:, i * 128 : i * 128 + 128] * keep).astype(BF16)
            bottom = (down[:, i * 128 : i * 128 + 128] * keep).astype(BF16)

            def put(ref, first):
                ref[place - first, : 2 * HID, :] = top
                ref[place - first, 2 * HID :, :] = bottom

            for ref, first, last in spans:
                pl.when((place >= first) & (place < last))(functools.partial(put, ref, first))


def slot_grad_kernel(table_ref, both_ref, *refs):
    del table_ref
    w_refs, out_ref = refs[:8], refs[8]
    both = both_ref[...]
    upper, _ = half_of_row((ROWS, 2 * HID), 0)
    zero = jnp.zeros_like(both)
    total = None
    for h in range(2):
        own = jnp.where(upper, both, zero) if h else jnp.where(upper, zero, both)
        part = lax.dot_general(
            own,
            stack_rows(w_refs[4 * h : 4 * h + 4], 0, 2 * HID),
            (((1,), (1,)), ((), ())),
            preferred_element_type=F32,
        )
        total = part if total is None else total + part
    out_ref[...] = total.astype(BF16)


def combine_kernel(back_ref, slots_ref, out_ref):
    step = pl.program_id(0)
    total = jnp.dot(back_ref[...], slots_ref[...], preferred_element_type=F32).astype(BF16)
    at = pl.multiple_of(step * COLS, COLS)
    out_ref[:, pl.ds(at, COLS)] = total[:TOK, :]
    out_ref[:, pl.ds(pl.multiple_of(at + HALF, COLS), COLS)] = total[TOK:, :]


def whole(shape):
    return pl.BlockSpec(shape, lambda i, *_: (0,) * len(shape))


def columns(rows, at=lambda i: i):
    return pl.BlockSpec((rows, COLS), lambda i, *_: (0, at(i)))


def weight_blocks():
    return [
        pl.BlockSpec(
            (1, 128, 3 * HID),
            lambda i, table, *_, first=BLOCKS // 2 * h + j: (
                table[4 * (jnp.minimum(i, 2 * STEPS - 1) % STEPS) + first],
                0,
                0,
            ),
        )
        for h in range(2)
        for j in range(4)
    ]


def call(kernel, steps, ins, outs, shapes, flops, nbytes, scratch=(), prefetch=0):
    return pl.pallas_call(
        kernel,
        grid_spec=pltpu.PrefetchScalarGridSpec(
            num_scalar_prefetch=prefetch,
            grid=(steps,),
            in_specs=ins,
            out_specs=outs,
            scratch_shapes=list(scratch),
        ),
        out_shape=shapes,
        compiler_params=pltpu.CompilerParams(dimension_semantics=("arbitrary",)),
        cost_estimate=pl.CostEstimate(flops=flops, bytes_accessed=nbytes, transcendentals=0),
    )


def sds(shape, dtype):
    return jax.ShapeDtypeStruct(shape, dtype)


def exchange(rows):
    return lax.all_to_all(
        rows.reshape(EXPERTS, 2 * CAP, -1), "exp", split_axis=0, concat_axis=0, tiled=True
    ).reshape(rows.shape)


def hop(value, distance):
    reps = lax.axis_size("rep")
    turn = [
        (i, (i + 2 * distance) % reps if i % 2 == 0 else (i - 2 * distance) % reps)
        for i in range(reps)
    ]
    return lax.ppermute(value, "rep", turn)


def swap(value):
    return lax.ppermute(value, "rep", [(i, i ^ 1) for i in range(lax.axis_size("rep"))])


def places(rep, sign):
    block = jnp.arange(BLOCKS, dtype=jnp.int32)
    core = rep & 1
    kind = block & 1
    ahead = (sign * ((block >> 1) - (rep >> 1))) & 15
    carrier = jnp.where(ahead == 8, kind, (ahead > 8).astype(jnp.int32))
    carrier = jnp.where(ahead == 0, core, carrier)
    distance = jnp.where(ahead > 8, 16 - ahead, ahead)
    odd = (distance & 1) == 1
    step = jnp.where(odd, distance, distance - 1)
    second = (kind != carrier).astype(jnp.int32)
    pair = 2 * ((step & 2) + ((step >> 2) & 1)) + second
    return distance == 0, odd, pair, second, carrier == core


def gathered_places(rep):
    here, odd, pair, second, local = places(rep, -1)
    at = jnp.where(here, second, jnp.where(odd, 2, 10) + pair)
    return jnp.where(local, at, at + 16)


def scattered_places(rep):
    here, odd, pair, second, local = places(rep, 1)
    at = jnp.where(here, 15 + second, jnp.where(odd, 7, 0) + pair)
    return jnp.where(local, at, at + 17)


def join_kernel(count, *refs):
    out, sems = refs[count:]
    copies, at = [], 0
    for i, piece in enumerate(refs[:count]):
        span = piece.shape[0]
        copies.append(pltpu.make_async_copy(piece, out.at[pl.ds(at, span)], sems.at[i]))
        copies[-1].start()
        at += span
    for copy in copies:
        copy.wait()


def join(pieces):
    blocks = sum(piece.shape[0] for piece in pieces)
    return pl.pallas_call(
        functools.partial(join_kernel, len(pieces)),
        in_specs=[pl.BlockSpec(memory_space=pl.ANY)] * len(pieces),
        out_specs=pl.BlockSpec(memory_space=pltpu.VMEM),
        out_shape=sds((blocks,) + pieces[0].shape[1:], pieces[0].dtype),
        scratch_shapes=[pltpu.SemaphoreType.DMA((len(pieces),))],
        cost_estimate=pl.CostEstimate(flops=0, bytes_accessed=8 << 20, transcendentals=0),
    )(*pieces)


def gather_weights(own):
    near = jnp.stack([own, swap(own)])
    one = hop(near, 1)
    five = hop(one, 4)
    three_seven = hop(jnp.concatenate([one, five]), 2)
    odd = jnp.concatenate([one, five, three_seven])
    even = hop(odd, 1)
    return join([near, odd, even, swap(odd), swap(even)])


def scatter_sum(even, odd, here, give_even, give_odd):
    def add(*parts):
        return functools.reduce(jnp.add, [part.astype(F32) for part in parts])

    one = hop(add(even, swap(give_even)).astype(BF16), 1)
    got = swap(give_odd)
    last = jnp.pad(one[4:], ((0, 1), (0, 0), (0, 0)))
    two = hop(add(odd[4:], got[4:], last).astype(BF16), 2)
    four = hop(add(odd[2:4], got[2:4], one[2:4], two[2:]).astype(BF16), 4)
    return hop(add(odd[:2], got[:2], one[:2], two[:2], four).astype(BF16), 1)


def per_device(tokens, grad_out, gates, expert_ids, w_all, touched):
    rep = lax.axis_index("rep")
    ids = expert_ids.T
    mbytes = 1 << 20
    early = lambda i: jnp.minimum(i, STEPS - 1)
    late = lambda i: jnp.maximum(i - STEPS, 0)
    sent = call(
        place_kernel,
        2 * STEPS,
        [
            whole((2, TOK)),
            whole((2, TOK)),
            columns(TOK, early),
            columns(TOK, lambda i: early(i) + STEPS),
            columns(TOK, late),
            columns(TOK, lambda i: late(i) + STEPS),
        ],
        columns(ROWS),
        sds((ROWS, WIDTH), BF16),
        4 * ROWS * 256 * HALF,
        8 * mbytes,
        [pltpu.VMEM((ROWS, 2 * TOK), BF16), pltpu.VMEM((ROWS, 128), F32)],
    )(ids, gates.T, tokens, tokens, grad_out, grad_out)
    received = exchange(sent)
    back = call(
        back_kernel, 1, [whole((2, TOK))], whole((2 * TOK, ROWS)), sds((2 * TOK, ROWS), BF16), 0, mbytes
    )(ids)
    w_whole = gather_weights(w_all[0])
    table = gathered_places(rep)
    info = jnp.concatenate([touched.reshape(-1), scattered_places(rep)])
    shares = [(n, 3 * HID, 128) for n in (7, 8, 2, 7, 8)]
    both_grad, even, odd, here, give_even, give_odd = call(
        expert_kernel,
        3 * STEPS,
        [pl.BlockSpec(memory_space=pl.ANY)] + weight_blocks(),
        [whole((ROWS, 2 * HID))] + [whole(share) for share in shares],
        [sds((ROWS, 2 * HID), BF16)] + [sds(share, BF16) for share in shares],
        2 * ROWS * HALF * 12 * HID,
        16 * mbytes,
        [
            pltpu.VMEM((ROWS, WIDTH), BF16),
            pltpu.VMEM((6 * HID, ROWS), BF16),
            pltpu.VMEM((ROWS, 4 * HID), F32),
            pltpu.VMEM((ROWS, 2 * HID), F32),
            pltpu.SemaphoreType.DMA((2 * STEPS,)),
        ],
        2,
    )(table, info, received, *[w_whole] * 8)
    final = scatter_sum(even, odd, here, give_even, give_odd)
    slot_grad = call(
        slot_grad_kernel,
        STEPS,
        [whole((ROWS, 2 * HID))] + weight_blocks(),
        columns(ROWS),
        sds((ROWS, HALF), BF16),
        2 * ROWS * HALF * 4 * HID,
        6 * mbytes,
        (),
        1,
    )(table, both_grad, *[w_whole] * 8)
    returned = exchange(slot_grad)
    token_grad = call(
        combine_kernel,
        STEPS,
        [whole((2 * TOK, ROWS)), columns(ROWS)],
        whole((TOK, WIDTH)),
        sds((TOK, WIDTH), BF16),
        2 * ROWS * 256 * HALF,
        4 * mbytes,
    )(back, returned)
    final, token_grad = lax.optimization_barrier((final, token_grad))
    total = here.astype(F32) + final.astype(F32)
    owned = total[:1] + swap(total[1:].astype(BF16)).astype(F32)
    return (token_grad, jnp.swapaxes(owned, 1, 2))


def solution(mesh):
    in_specs = (
        P(("rep", "exp"), None),
        P(("rep", "exp"), None),
        P(("rep", "exp"), None),
        P(("rep", "exp"), None),
        P("exp", "rep", None),
        P("rep", "exp", None),
    )
    out_specs = (P(("rep", "exp"), None), P("exp", "rep", None))
    return jax.shard_map(
        per_device, mesh=mesh, in_specs=in_specs, out_specs=out_specs, check_vma=False
    )
```

```python
import functools

import jax
import jax.numpy as jnp
from jax import lax
from jax.experimental import pallas as pl
from jax.experimental.pallas import tpu as pltpu
from jax.sharding import PartitionSpec as P


BF16 = jnp.bfloat16
F32 = jnp.float32
TOK, WIDTH, EXPERTS, CAP, HID = 128, 4096, 16, 20, 128
HALF = WIDTH // 2
ROWS = 2 * EXPERTS * CAP
STEPS = 4
COLS = HALF // STEPS
BLOCKS = WIDTH // 128


def half_of_row(shape, axis):
    row = lax.broadcasted_iota(jnp.int32, shape, axis)
    group = (row * 1639) >> 16
    rest = row - group * (2 * CAP)
    upper = rest >= CAP
    return upper, group * CAP + jnp.where(upper, rest - CAP, rest)


def targets(ids):
    expert = lax.broadcasted_iota(jnp.int32, (EXPERTS, TOK), 0)
    first = (jnp.broadcast_to(ids[0:1, :], (EXPERTS, TOK)) == expert).astype(F32)
    second = (jnp.broadcast_to(ids[1:2, :], (EXPERTS, TOK)) == expert).astype(F32)
    earlier = lax.broadcasted_iota(jnp.int32, (TOK, TOK), 0) < lax.broadcasted_iota(
        jnp.int32, (TOK, TOK), 1
    )
    before = jnp.dot(
        (first + second).astype(BF16),
        earlier.astype(F32).astype(BF16),
        preferred_element_type=F32,
    )
    rank0 = jnp.sum(first * before, 0, keepdims=True).astype(jnp.int32)
    rank1 = jnp.sum(second * before, 0, keepdims=True).astype(jnp.int32)
    return ids[0:1, :] * CAP + rank0, ids[1:2, :] * CAP + rank1


def hits(ids):
    target0, target1 = targets(ids)
    upper, slot = half_of_row((ROWS, TOK), 0)
    hit0 = slot == jnp.broadcast_to(target0, (ROWS, TOK))
    hit1 = slot == jnp.broadcast_to(target1, (ROWS, TOK))
    return hit0, hit1, upper


def placement(hit0, hit1, upper):
    hit = jnp.where(hit0 | hit1, 1.0, 0.0)
    return jnp.concatenate([jnp.where(upper, 0.0, hit), jnp.where(upper, hit, 0.0)], 1)


def place_kernel(
    ids_ref, gates_ref, x_low_ref, x_high_ref, dy_low_ref, dy_high_ref, out_ref, place, gate
):
    step = pl.program_id(0)

    @pl.when(step == 0)
    def _():
        place[...] = placement(*hits(ids_ref[...])).astype(BF16)

    @pl.when(step < STEPS)
    def _():
        both = jnp.concatenate([x_low_ref[...], x_high_ref[...]], 0)
        out_ref[...] = jnp.dot(place[...], both, preferred_element_type=F32).astype(BF16)

    @pl.when(step == STEPS)
    def _():
        hit0, hit1, _ = hits(ids_ref[...])
        gates = gates_ref[...]
        weight = jnp.where(hit0, jnp.broadcast_to(gates[0:1, :], (ROWS, TOK)), 0.0) + jnp.where(
            hit1, jnp.broadcast_to(gates[1:2, :], (ROWS, TOK)), 0.0
        )
        gate[...] = jnp.broadcast_to(jnp.sum(weight, 1, keepdims=True), (ROWS, 128))

    @pl.when(step >= STEPS)
    def _():
        both = jnp.concatenate([dy_low_ref[...], dy_high_ref[...]], 0)
        picked = jnp.dot(place[...], both, preferred_element_type=F32)
        scale = gate[...]
        for i in range(COLS // 128):
            part = picked[:, i * 128 : i * 128 + 128] * scale
            out_ref[:, i * 128 : i * 128 + 128] = part.astype(BF16)


def back_kernel(ids_ref, back_ref):
    back_ref[...] = placement(*hits(ids_ref[...])).T.astype(BF16)


def join_halves(acc, width):
    upper, _ = half_of_row((ROWS, width), 0)
    own = jnp.where(upper, acc[:, width:], acc[:, :width])
    other = jnp.where(upper, pltpu.roll(own, CAP, 0), pltpu.roll(own, ROWS - CAP, 0))
    return own + other


def stack_rows(table_ref, weights, step, h, start, stop):
    first = 4 * step + BLOCKS // 2 * h
    return jnp.concatenate([weights[table_ref[first + j], :, start:stop] for j in range(4)], 0)


def piece_copies(pieces, weights, sems):
    copies, at = [], 0
    for i, piece in enumerate(pieces):
        span = piece.shape[0]
        copies.append(pltpu.make_async_copy(piece, weights.at[pl.ds(at, span)], sems.at[i]))
        at += span
    return copies


def column_copy(recv_ref, slots, sems, i):
    at = pl.ds(pl.multiple_of(i * COLS, COLS), COLS)
    return pltpu.make_async_copy(recv_ref.at[:, at], slots.at[:, at], sems.at[i])


def expert_kernel(table_ref, info_ref, recv_ref, *refs):
    gathered, both_ref, pieces = refs[:5], refs[5], refs[6:11]
    slots, weights, turned_ref, gate_up, down, sems, w_sems = refs[11:]
    step = pl.program_id(0)

    @pl.when(step == 0)
    def _():
        copies = piece_copies(gathered, weights, w_sems)
        for copy in copies:
            copy.start()
        for i in range(2 * STEPS):
            column_copy(recv_ref, slots, sems, i).start()
        gate_up[...] = jnp.zeros_like(gate_up)
        down[...] = jnp.zeros_like(down)
        for copy in copies:
            copy.wait()

    @pl.when(step < 2 * STEPS)
    def _():
        column_copy(recv_ref, slots, sems, step).wait()

    @pl.when(step < STEPS)
    def _():
        x = slots[:, pl.ds(pl.multiple_of(step * COLS, COLS), COLS)]
        for h in range(2):
            gate_up[:, 2 * HID * h : 2 * HID * (h + 1)] += jnp.dot(
                x,
                stack_rows(table_ref, weights, step, h, 0, 2 * HID),
                preferred_element_type=F32,
            )

    @pl.when((step >= STEPS) & (step < 2 * STEPS))
    def _():
        dy = slots[:, pl.ds(pl.multiple_of(step * COLS, COLS), COLS)]
        w_down = [
            stack_rows(table_ref, weights, step - STEPS, h, 2 * HID, 3 * HID) for h in range(2)
        ]
        down[...] += jnp.dot(dy, jnp.concatenate(w_down, 1), preferred_element_type=F32)

    @pl.when(step == 2 * STEPS - 1)
    def _():
        joined = join_halves(gate_up[...], 2 * HID)
        hid_grad = join_halves(down[...], HID)
        gate_pre = joined[:, :HID]
        up_pre = joined[:, HID:]
        sigmoid_g = jax.nn.sigmoid(gate_pre)
        silu_val = gate_pre * sigmoid_g
        silu_slope = sigmoid_g * (1.0 + gate_pre * (1.0 - sigmoid_g))
        gate_grad = hid_grad * up_pre * silu_slope
        up_grad = hid_grad * silu_val
        hidden = silu_val * up_pre
        both_ref[:, :HID] = gate_grad.astype(BF16)
        both_ref[:, HID:] = up_grad.astype(BF16)
        upper, _ = half_of_row((HID, ROWS), 1)
        for i, value in enumerate((gate_grad, up_grad, hidden)):
            turned = value.T
            turned_ref[i * HID : (i + 1) * HID, :] = jnp.where(upper, 0.0, turned).astype(BF16)
            turned_ref[(i + 3) * HID : (i + 4) * HID, :] = jnp.where(upper, turned, 0.0).astype(
                BF16
            )

    @pl.when(step >= 2 * STEPS)
    def _():
        weight_grad(info_ref, step - 2 * STEPS, slots, turned_ref, pieces)


def weight_grad(info_ref, step, slots, turned_ref, pieces):
    at = pl.multiple_of(step * COLS, COLS)
    x = slots[:, pl.ds(at, COLS)]
    dy = slots[:, pl.ds(pl.multiple_of(at + HALF, COLS), COLS)]
    spans = tuple(zip(pieces, (0, 7, 15, 17, 24), (7, 15, 17, 24, 32)))
    for h in range(2):
        base = 3 * HID * h
        proj = jnp.dot(turned_ref[base : base + 2 * HID, :], x, preferred_element_type=F32)
        down = jnp.dot(
            turned_ref[base + 2 * HID : base + 3 * HID, :], dy, preferred_element_type=F32
        )
        for i in range(COLS // 128):
            block = step * (COLS // 128) + i + h * (BLOCKS // 2)
            keep = info_ref[block].astype(F32)
            place = info_ref[BLOCKS + block]
            top = (proj[:, i * 128 : i * 128 + 128] * keep).astype(BF16)
            bottom = (down[:, i * 128 : i * 128 + 128] * keep).astype(BF16)

            def put(ref, first):
                ref[place - first, : 2 * HID, :] = top
                ref[place - first, 2 * HID :, :] = bottom

            for ref, first, last in spans:
                pl.when((place >= first) & (place < last))(functools.partial(put, ref, first))


def slot_grad_kernel(table_ref, both_ref, *refs):
    gathered, (out_ref, weights, w_sems) = refs[:5], refs[5:]
    step = pl.program_id(0)

    @pl.when(step == 0)
    def _():
        copies = piece_copies(gathered, weights, w_sems)
        for copy in copies:
            copy.start()
        for copy in copies:
            copy.wait()

    both = both_ref[...]
    upper, _ = half_of_row((ROWS, 2 * HID), 0)
    zero = jnp.zeros_like(both)
    total = None
    for h in range(2):
        own = jnp.where(upper, both, zero) if h else jnp.where(upper, zero, both)
        part = lax.dot_general(
            own,
            stack_rows(table_ref, weights, step, h, 0, 2 * HID),
            (((1,), (1,)), ((), ())),
            preferred_element_type=F32,
        )
        total = part if total is None else total + part
    out_ref[...] = total.astype(BF16)


def combine_kernel(back_ref, slots_ref, out_ref):
    step = pl.program_id(0)
    total = jnp.dot(back_ref[...], slots_ref[...], preferred_element_type=F32).astype(BF16)
    at = pl.multiple_of(step * COLS, COLS)
    out_ref[:, pl.ds(at, COLS)] = total[:TOK, :]
    out_ref[:, pl.ds(pl.multiple_of(at + HALF, COLS), COLS)] = total[TOK:, :]


def whole(shape):
    return pl.BlockSpec(shape, lambda i, *_: (0,) * len(shape))


def columns(rows, at=lambda i: i):
    return pl.BlockSpec((rows, COLS), lambda i, *_: (0, at(i)))


def call(kernel, steps, ins, outs, shapes, flops, nbytes, scratch=(), prefetch=0):
    return pl.pallas_call(
        kernel,
        grid_spec=pltpu.PrefetchScalarGridSpec(
            num_scalar_prefetch=prefetch,
            grid=(steps,),
            in_specs=ins,
            out_specs=outs,
            scratch_shapes=list(scratch),
        ),
        out_shape=shapes,
        compiler_params=pltpu.CompilerParams(dimension_semantics=("arbitrary",)),
        cost_estimate=pl.CostEstimate(flops=flops, bytes_accessed=nbytes, transcendentals=0),
    )


def sds(shape, dtype):
    return jax.ShapeDtypeStruct(shape, dtype)


def exchange(rows):
    return lax.all_to_all(
        rows.reshape(EXPERTS, 2 * CAP, -1), "exp", split_axis=0, concat_axis=0, tiled=True
    ).reshape(rows.shape)


def hop(value, distance):
    reps = lax.axis_size("rep")
    turn = [
        (i, (i + 2 * distance) % reps if i % 2 == 0 else (i - 2 * distance) % reps)
        for i in range(reps)
    ]
    return lax.ppermute(value, "rep", turn)


def swap(value):
    return lax.ppermute(value, "rep", [(i, i ^ 1) for i in range(lax.axis_size("rep"))])


def places(rep, sign):
    block = jnp.arange(BLOCKS, dtype=jnp.int32)
    core = rep & 1
    kind = block & 1
    ahead = (sign * ((block >> 1) - (rep >> 1))) & 15
    carrier = jnp.where(ahead == 8, kind, (ahead > 8).astype(jnp.int32))
    carrier = jnp.where(ahead == 0, core, carrier)
    distance = jnp.where(ahead > 8, 16 - ahead, ahead)
    odd = (distance & 1) == 1
    step = jnp.where(odd, distance, distance - 1)
    second = (kind != carrier).astype(jnp.int32)
    pair = 2 * ((step & 2) + ((step >> 2) & 1)) + second
    return distance == 0, odd, pair, second, carrier == core


def gathered_places(rep):
    here, odd, pair, second, local = places(rep, -1)
    at = jnp.where(here, second, jnp.where(odd, 2, 10) + pair)
    return jnp.where(local, at, at + 16)


def scattered_places(rep):
    here, odd, pair, second, local = places(rep, 1)
    at = jnp.where(here, 15 + second, jnp.where(odd, 7, 0) + pair)
    return jnp.where(local, at, at + 17)


def gather_weights(own):
    near = jnp.stack([own, swap(own)])
    one = hop(near, 1)
    five = hop(one, 4)
    three_seven = hop(jnp.concatenate([one, five]), 2)
    odd = jnp.concatenate([one, five, three_seven])
    even = hop(odd, 1)
    return near, odd, even, swap(odd), swap(even)


def scatter_sum(even, odd, give_odd):
    def add(*parts):
        return functools.reduce(jnp.add, [part.astype(F32) for part in parts])

    one = hop(even, 1)
    got = swap(give_odd)
    last = lax.pad(one, jnp.zeros((), BF16), ((-4, 1, 0), (0, 0, 0), (0, 0, 0)))
    second = add(odd[4:], got[4:], last).astype(BF16)
    two = hop(second, 2)
    four = hop(add(odd[2:4], got[2:4], one[2:4], two[2:]).astype(BF16), 4)
    return hop(add(odd[:2], got[:2], one[:2], two[:2], four).astype(BF16), 1)


def per_device(tokens, grad_out, gates, expert_ids, w_all, touched):
    rep = lax.axis_index("rep")
    ids = expert_ids.T
    mbytes = 1 << 20
    early = lambda i: jnp.minimum(i, STEPS - 1)
    late = lambda i: jnp.maximum(i - STEPS, 0)
    sent = call(
        place_kernel,
        2 * STEPS,
        [
            whole((2, TOK)),
            whole((2, TOK)),
            columns(TOK, early),
            columns(TOK, lambda i: early(i) + STEPS),
            columns(TOK, late),
            columns(TOK, lambda i: late(i) + STEPS),
        ],
        columns(ROWS),
        sds((ROWS, WIDTH), BF16),
        4 * ROWS * 256 * HALF,
        8 * mbytes,
        [pltpu.VMEM((ROWS, 2 * TOK), BF16), pltpu.VMEM((ROWS, 128), F32)],
    )(ids, gates.T, tokens, tokens, grad_out, grad_out)
    received = exchange(sent)
    back = call(
        back_kernel,
        1,
        [whole((2, TOK))],
        whole((2 * TOK, ROWS)),
        sds((2 * TOK, ROWS), BF16),
        0,
        mbytes,
    )(ids)
    gathered = gather_weights(w_all[0])
    in_place = [pl.BlockSpec(memory_space=pl.ANY)]
    weights = [
        pltpu.VMEM((sum(piece.shape[0] for piece in gathered), 128, 3 * HID), BF16),
        pltpu.SemaphoreType.DMA((len(gathered),)),
    ]
    table = gathered_places(rep)
    info = jnp.concatenate([touched.reshape(-1), scattered_places(rep)])
    shares = [(n, 3 * HID, 128) for n in (7, 8, 2, 7, 8)]
    both_grad, even, odd, here, give_even, give_odd = call(
        expert_kernel,
        3 * STEPS,
        in_place * 6,
        [whole((ROWS, 2 * HID))] + [whole(share) for share in shares],
        [sds((ROWS, 2 * HID), BF16)] + [sds(share, BF16) for share in shares],
        2 * ROWS * HALF * 12 * HID,
        16 * mbytes,
        [
            pltpu.VMEM((ROWS, WIDTH), BF16),
            weights[0],
            pltpu.VMEM((6 * HID, ROWS), BF16),
            pltpu.VMEM((ROWS, 4 * HID), F32),
            pltpu.VMEM((ROWS, 2 * HID), F32),
            pltpu.SemaphoreType.DMA((2 * STEPS,)),
            weights[1],
        ],
        2,
    )(table, info, received, *gathered)
    paired = (even.astype(F32) + swap(give_even).astype(F32)).astype(BF16)
    paired, both_grad, give_odd = lax.optimization_barrier((paired, both_grad, give_odd))
    final = scatter_sum(paired, odd, give_odd)
    slot_grad = call(
        slot_grad_kernel,
        STEPS,
        [whole((ROWS, 2 * HID))] + in_place * 5,
        columns(ROWS),
        sds((ROWS, HALF), BF16),
        2 * ROWS * HALF * 4 * HID,
        6 * mbytes,
        weights,
        1,
    )(table, both_grad, *gathered)
    returned = exchange(slot_grad)
    token_grad = call(
        combine_kernel,
        STEPS,
        [whole((2 * TOK, ROWS)), columns(ROWS)],
        whole((TOK, WIDTH)),
        sds((TOK, WIDTH), BF16),
        2 * ROWS * 256 * HALF,
        4 * mbytes,
    )(back, returned)
    final, token_grad = lax.optimization_barrier((final, token_grad))
    total = here.astype(F32) + final.astype(F32)
    owned = total[:1] + swap(total[1:].astype(BF16)).astype(F32)
    return (token_grad, jnp.swapaxes(owned, 1, 2))


def solution(mesh):
    in_specs = (
        P(("rep", "exp"), None),
        P(("rep", "exp"), None),
        P(("rep", "exp"), None),
        P(("rep", "exp"), None),
        P("exp", "rep", None),
        P("rep", "exp", None),
    )
    out_specs = (P(("rep", "exp"), None), P("exp", "rep", None))

    return jax.shard_map(
        per_device, mesh=mesh, in_specs=in_specs, out_specs=out_specs, check_vma=False
    )
```

```python
import functools

import jax
import jax.numpy as jnp
from jax import lax
from jax.experimental import pallas as pl
from jax.experimental.pallas import tpu as pltpu
from jax.sharding import PartitionSpec as P


BF16 = jnp.bfloat16
F32 = jnp.float32
TOK, WIDTH, EXPERTS, CAP, HID = 128, 4096, 16, 20, 128
HALF = WIDTH // 2
ROWS = 2 * EXPERTS * CAP
STEPS = 4
COLS = HALF // STEPS
BLOCKS = WIDTH // 128


def half_of_row(shape, axis):
    row = lax.broadcasted_iota(jnp.int32, shape, axis)
    group = (row * 1639) >> 16
    rest = row - group * (2 * CAP)
    upper = rest >= CAP
    return upper, group * CAP + jnp.where(upper, rest - CAP, rest)


def targets(ids):
    expert = lax.broadcasted_iota(jnp.int32, (EXPERTS, TOK), 0)
    first = (jnp.broadcast_to(ids[0:1, :], (EXPERTS, TOK)) == expert).astype(F32)
    second = (jnp.broadcast_to(ids[1:2, :], (EXPERTS, TOK)) == expert).astype(F32)
    earlier = lax.broadcasted_iota(jnp.int32, (TOK, TOK), 0) < lax.broadcasted_iota(
        jnp.int32, (TOK, TOK), 1
    )
    before = jnp.dot(
        (first + second).astype(BF16),
        earlier.astype(F32).astype(BF16),
        preferred_element_type=F32,
    )
    rank0 = jnp.sum(first * before, 0, keepdims=True).astype(jnp.int32)
    rank1 = jnp.sum(second * before, 0, keepdims=True).astype(jnp.int32)
    return ids[0:1, :] * CAP + rank0, ids[1:2, :] * CAP + rank1


def hits(ids):
    target0, target1 = targets(ids)
    upper, slot = half_of_row((ROWS, TOK), 0)
    hit0 = slot == jnp.broadcast_to(target0, (ROWS, TOK))
    hit1 = slot == jnp.broadcast_to(target1, (ROWS, TOK))
    return hit0, hit1, upper


def placement(hit0, hit1, upper):
    hit = jnp.where(hit0 | hit1, 1.0, 0.0)
    return jnp.concatenate([jnp.where(upper, 0.0, hit), jnp.where(upper, hit, 0.0)], 1)


def place_kernel(
    ids_ref, gates_ref, x_low_ref, x_high_ref, dy_low_ref, dy_high_ref, out_ref, place, gate
):
    step = pl.program_id(0)

    @pl.when(step == 0)
    def _():
        place[...] = placement(*hits(ids_ref[...])).astype(BF16)

    @pl.when(step < STEPS)
    def _():
        both = jnp.concatenate([x_low_ref[...], x_high_ref[...]], 0)
        out_ref[...] = jnp.dot(place[...], both, preferred_element_type=F32).astype(BF16)

    @pl.when(step == STEPS)
    def _():
        hit0, hit1, _ = hits(ids_ref[...])
        gates = gates_ref[...]
        weight = jnp.where(hit0, jnp.broadcast_to(gates[0:1, :], (ROWS, TOK)), 0.0) + jnp.where(
            hit1, jnp.broadcast_to(gates[1:2, :], (ROWS, TOK)), 0.0
        )
        gate[...] = jnp.broadcast_to(jnp.sum(weight, 1, keepdims=True), (ROWS, 128))

    @pl.when(step >= STEPS)
    def _():
        both = jnp.concatenate([dy_low_ref[...], dy_high_ref[...]], 0)
        picked = jnp.dot(place[...], both, preferred_element_type=F32)
        scale = gate[...]
        for i in range(COLS // 128):
            part = picked[:, i * 128 : i * 128 + 128] * scale
            out_ref[:, i * 128 : i * 128 + 128] = part.astype(BF16)


def back_kernel(ids_ref, back_ref):
    back_ref[...] = placement(*hits(ids_ref[...])).T.astype(BF16)


def join_halves(acc, width):
    upper, _ = half_of_row((ROWS, width), 0)
    own = jnp.where(upper, acc[:, width:], acc[:, :width])
    other = jnp.where(upper, pltpu.roll(own, CAP, 0), pltpu.roll(own, ROWS - CAP, 0))
    return own + other


def stack_rows(table_ref, weights, step, h, start, stop):
    first = 4 * step + BLOCKS // 2 * h
    return jnp.concatenate([weights[table_ref[first + j], :, start:stop] for j in range(4)], 0)


def piece_copies(pieces, weights, sems):
    copies, at = [], 0
    for i, piece in enumerate(pieces):
        span = piece.shape[0]
        copies.append(pltpu.make_async_copy(piece, weights.at[pl.ds(at, span)], sems.at[i]))
        at += span
    return copies


def column_copy(recv_ref, slots, sems, i):
    at = pl.ds(pl.multiple_of(i * COLS, COLS), COLS)
    return pltpu.make_async_copy(recv_ref.at[:, at], slots.at[:, at], sems.at[i])


def expert_kernel(table_ref, info_ref, recv_ref, *refs):
    gathered, both_ref, pieces = refs[:5], refs[5], refs[6:10]
    slots, weights, turned_ref, gate_up, down, sems, w_sems = refs[10:]
    step = pl.program_id(0)

    @pl.when(step == 0)
    def _():
        copies = piece_copies(gathered, weights, w_sems)
        for copy in copies:
            copy.start()
        for i in range(2 * STEPS):
            column_copy(recv_ref, slots, sems, i).start()
        gate_up[...] = jnp.zeros_like(gate_up)
        down[...] = jnp.zeros_like(down)
        for copy in copies:
            copy.wait()

    @pl.when(step < 2 * STEPS)
    def _():
        column_copy(recv_ref, slots, sems, step).wait()

    @pl.when(step < STEPS)
    def _():
        x = slots[:, pl.ds(pl.multiple_of(step * COLS, COLS), COLS)]
        for h in range(2):
            gate_up[:, 2 * HID * h : 2 * HID * (h + 1)] += jnp.dot(
                x,
                stack_rows(table_ref, weights, step, h, 0, 2 * HID),
                preferred_element_type=F32,
            )

    @pl.when((step >= STEPS) & (step < 2 * STEPS))
    def _():
        dy = slots[:, pl.ds(pl.multiple_of(step * COLS, COLS), COLS)]
        w_down = [
            stack_rows(table_ref, weights, step - STEPS, h, 2 * HID, 3 * HID) for h in range(2)
        ]
        down[...] += jnp.dot(dy, jnp.concatenate(w_down, 1), preferred_element_type=F32)

    @pl.when(step == 2 * STEPS - 1)
    def _():
        joined = join_halves(gate_up[...], 2 * HID)
        hid_grad = join_halves(down[...], HID)
        gate_pre = joined[:, :HID]
        up_pre = joined[:, HID:]
        sigmoid_g = jax.nn.sigmoid(gate_pre)
        silu_val = gate_pre * sigmoid_g
        silu_slope = sigmoid_g * (1.0 + gate_pre * (1.0 - sigmoid_g))
        gate_grad = hid_grad * up_pre * silu_slope
        up_grad = hid_grad * silu_val
        hidden = silu_val * up_pre
        both_ref[:, :HID] = gate_grad.astype(BF16)
        both_ref[:, HID:] = up_grad.astype(BF16)
        upper, _ = half_of_row((HID, ROWS), 1)
        for i, value in enumerate((gate_grad, up_grad, hidden)):
            turned = value.T
            turned_ref[i * HID : (i + 1) * HID, :] = jnp.where(upper, 0.0, turned).astype(BF16)
            turned_ref[(i + 3) * HID : (i + 4) * HID, :] = jnp.where(upper, turned, 0.0).astype(
                BF16
            )

    @pl.when(step >= 2 * STEPS)
    def _():
        weight_grad(info_ref, step - 2 * STEPS, slots, turned_ref, pieces)


def weight_grad(info_ref, step, slots, turned_ref, pieces):
    at = pl.multiple_of(step * COLS, COLS)
    x = slots[:, pl.ds(at, COLS)]
    dy = slots[:, pl.ds(pl.multiple_of(at + HALF, COLS), COLS)]
    spans = tuple(zip(pieces, (0, 8, 16, 24), (8, 16, 24, 32)))
    for h in range(2):
        base = 3 * HID * h
        proj = jnp.dot(turned_ref[base : base + 2 * HID, :], x, preferred_element_type=F32)
        down = jnp.dot(
            turned_ref[base + 2 * HID : base + 3 * HID, :], dy, preferred_element_type=F32
        )
        for i in range(COLS // 128):
            block = step * (COLS // 128) + i + h * (BLOCKS // 2)
            keep = info_ref[block].astype(F32)
            place = info_ref[BLOCKS + block]
            top = (proj[:, i * 128 : i * 128 + 128] * keep).astype(BF16)
            bottom = (down[:, i * 128 : i * 128 + 128] * keep).astype(BF16)

            def put(ref, first):
                ref[place - first, : 2 * HID, :] = top
                ref[place - first, 2 * HID :, :] = bottom

            for ref, first, last in spans:
                pl.when((place >= first) & (place < last))(functools.partial(put, ref, first))


def slot_grad_kernel(table_ref, both_ref, *refs):
    gathered, (out_ref, weights, w_sems) = refs[:5], refs[5:]
    step = pl.program_id(0)

    @pl.when(step == 0)
    def _():
        copies = piece_copies(gathered, weights, w_sems)
        for copy in copies:
            copy.start()
        for copy in copies:
            copy.wait()

    both = both_ref[...]
    upper, _ = half_of_row((ROWS, 2 * HID), 0)
    zero = jnp.zeros_like(both)
    total = None
    for h in range(2):
        own = jnp.where(upper, both, zero) if h else jnp.where(upper, zero, both)
        part = lax.dot_general(
            own,
            stack_rows(table_ref, weights, step, h, 0, 2 * HID),
            (((1,), (1,)), ((), ())),
            preferred_element_type=F32,
        )
        total = part if total is None else total + part
    out_ref[...] = total.astype(BF16)


def combine_kernel(back_ref, slots_ref, out_ref):
    step = pl.program_id(0)
    total = jnp.dot(back_ref[...], slots_ref[...], preferred_element_type=F32).astype(BF16)
    at = pl.multiple_of(step * COLS, COLS)
    out_ref[:, pl.ds(at, COLS)] = total[:TOK, :]
    out_ref[:, pl.ds(pl.multiple_of(at + HALF, COLS), COLS)] = total[TOK:, :]


def whole(shape):
    return pl.BlockSpec(shape, lambda i, *_: (0,) * len(shape))


def columns(rows, at=lambda i: i):
    return pl.BlockSpec((rows, COLS), lambda i, *_: (0, at(i)))


def call(kernel, steps, ins, outs, shapes, flops, nbytes, scratch=(), prefetch=0):
    return pl.pallas_call(
        kernel,
        grid_spec=pltpu.PrefetchScalarGridSpec(
            num_scalar_prefetch=prefetch,
            grid=(steps,),
            in_specs=ins,
            out_specs=outs,
            scratch_shapes=list(scratch),
        ),
        out_shape=shapes,
        compiler_params=pltpu.CompilerParams(dimension_semantics=("arbitrary",)),
        cost_estimate=pl.CostEstimate(flops=flops, bytes_accessed=nbytes, transcendentals=0),
    )


def sds(shape, dtype):
    return jax.ShapeDtypeStruct(shape, dtype)


def exchange(rows):
    return lax.all_to_all(
        rows.reshape(EXPERTS, 2 * CAP, -1), "exp", split_axis=0, concat_axis=0, tiled=True
    ).reshape(rows.shape)


def hop(value, distance):
    reps = lax.axis_size("rep")
    turn = [
        (i, (i + 2 * distance) % reps if i % 2 == 0 else (i - 2 * distance) % reps)
        for i in range(reps)
    ]
    return lax.ppermute(value, "rep", turn)


def swap(value):
    return lax.ppermute(value, "rep", [(i, i ^ 1) for i in range(lax.axis_size("rep"))])


def gathered_places(rep):
    block = jnp.arange(BLOCKS, dtype=jnp.int32)
    core = rep & 1
    kind = block & 1
    behind = ((rep >> 1) - (block >> 1)) & 15
    carrier = jnp.where(behind == 8, kind, (behind > 8).astype(jnp.int32))
    carrier = jnp.where(behind == 0, core, carrier)
    distance = jnp.where(behind > 8, 16 - behind, behind)
    odd = (distance & 1) == 1
    step = jnp.where(odd, distance, distance - 1)
    second = (kind != carrier).astype(jnp.int32)
    pair = 2 * ((step & 2) + ((step >> 2) & 1)) + second
    at = jnp.where(behind == 0, second, jnp.where(odd, 2, 10) + pair)
    return jnp.where(carrier == core, at, at + 16)


def scattered_places(rep):
    block = jnp.arange(BLOCKS, dtype=jnp.int32)
    ahead = ((block >> 1) - (rep >> 1)) & 15
    index = ahead >> 2
    rest = ahead & 3
    at = jnp.where(rest == 1, index, jnp.where(rest == 2, 8 + index, 12 + index))
    at = jnp.where(rest == 3, 4 + ((index + 1) & 3), at)
    return jnp.where((block & 1) == (rep & 1), at, at + 16)


def shift(value, distance):
    reps = lax.axis_size("rep")
    return lax.ppermute(value, "rep", [(i, (i + 2 * distance) % reps) for i in range(reps)])


def gather_weights(own):
    near = jnp.stack([own, swap(own)])
    one = hop(near, 1)
    five = hop(one, 4)
    three_seven = hop(jnp.concatenate([one, five]), 2)
    odd = jnp.concatenate([one, five, three_seven])
    even = hop(odd, 1)
    return near, odd, even, swap(odd), swap(even)


def add(*parts):
    return functools.reduce(jnp.add, [part.astype(F32) for part in parts])


def per_device(tokens, grad_out, gates, expert_ids, w_all, touched):
    rep = lax.axis_index("rep")
    ids = expert_ids.T
    mbytes = 1 << 20
    early = lambda i: jnp.minimum(i, STEPS - 1)
    late = lambda i: jnp.maximum(i - STEPS, 0)
    sent = call(
        place_kernel,
        2 * STEPS,
        [
            whole((2, TOK)),
            whole((2, TOK)),
            columns(TOK, early),
            columns(TOK, lambda i: early(i) + STEPS),
            columns(TOK, late),
            columns(TOK, lambda i: late(i) + STEPS),
        ],
        columns(ROWS),
        sds((ROWS, WIDTH), BF16),
        4 * ROWS * 256 * HALF,
        8 * mbytes,
        [pltpu.VMEM((ROWS, 2 * TOK), BF16), pltpu.VMEM((ROWS, 128), F32)],
    )(ids, gates.T, tokens, tokens, grad_out, grad_out)
    received = exchange(sent)
    back = call(
        back_kernel,
        1,
        [whole((2, TOK))],
        whole((2 * TOK, ROWS)),
        sds((2 * TOK, ROWS), BF16),
        0,
        mbytes,
    )(ids)
    gathered = gather_weights(w_all[0])
    in_place = [pl.BlockSpec(memory_space=pl.ANY)]
    weights = [
        pltpu.VMEM((sum(piece.shape[0] for piece in gathered), 128, 3 * HID), BF16),
        pltpu.SemaphoreType.DMA((len(gathered),)),
    ]
    table = gathered_places(rep)
    info = jnp.concatenate([touched.reshape(-1), scattered_places(rep)])
    shares = [(8, 3 * HID, 128)] * 4
    both_grad, sides, rest, give_sides, give_rest = call(
        expert_kernel,
        3 * STEPS,
        in_place * 6,
        [whole((ROWS, 2 * HID))] + [whole(share) for share in shares],
        [sds((ROWS, 2 * HID), BF16)] + [sds(share, BF16) for share in shares],
        2 * ROWS * HALF * 12 * HID,
        16 * mbytes,
        [
            pltpu.VMEM((ROWS, WIDTH), BF16),
            weights[0],
            pltpu.VMEM((6 * HID, ROWS), BF16),
            pltpu.VMEM((ROWS, 4 * HID), F32),
            pltpu.VMEM((ROWS, 2 * HID), F32),
            pltpu.SemaphoreType.DMA((2 * STEPS,)),
            weights[1],
        ],
        2,
    )(table, info, received, *gathered)
    got = swap(give_sides)
    above = add(sides[:4], got[:4]).astype(BF16)
    below = add(sides[4:], got[4:]).astype(BF16)
    above, below, both_grad, give_rest = lax.optimization_barrier(
        (above, below, both_grad, give_rest)
    )
    from_below = shift(above, 1)
    from_above = shift(below, -1)
    got = swap(give_rest)
    two_above = add(rest[:2], got[:2]).astype(BF16)
    two_below = add(rest[2:4], got[2:4]).astype(BF16)
    two_below, two_above = shift(two_above, 2), shift(two_below, -2)
    near = [add(rest[4 + i], got[4 + i], from_below[i], from_above[i]) for i in range(4)]
    far = [
        shift((near[1] + two_below[1].astype(F32)).astype(BF16), 4),
        shift(near[2].astype(BF16), 8),
        shift((near[3] + two_above[0].astype(F32)).astype(BF16), -4),
    ]
    near = add(near[0], two_below[0], two_above[1])
    slot_grad = call(
        slot_grad_kernel,
        STEPS,
        [whole((ROWS, 2 * HID))] + in_place * 5,
        columns(ROWS),
        sds((ROWS, HALF), BF16),
        2 * ROWS * HALF * 4 * HID,
        6 * mbytes,
        weights,
        1,
    )(table, both_grad, *gathered)
    returned = exchange(slot_grad)
    token_grad = call(
        combine_kernel,
        STEPS,
        [whole((2 * TOK, ROWS)), columns(ROWS)],
        whole((TOK, WIDTH)),
        sds((TOK, WIDTH), BF16),
        2 * ROWS * 256 * HALF,
        4 * mbytes,
    )(back, returned)
    far, token_grad = lax.optimization_barrier((far, token_grad))
    return (token_grad, add(near, *far).T[None])


def solution(mesh):
    in_specs = (
        P(("rep", "exp"), None),
        P(("rep", "exp"), None),
        P(("rep", "exp"), None),
        P(("rep", "exp"), None),
        P("exp", "rep", None),
        P("rep", "exp", None),
    )
    out_specs = (P(("rep", "exp"), None), P("exp", "rep", None))

    return jax.shard_map(
        per_device, mesh=mesh, in_specs=in_specs, out_specs=out_specs, check_vma=False
    )
```

```python
import functools

import jax
import jax.numpy as jnp
from jax import lax
from jax.experimental import pallas as pl
from jax.experimental.pallas import tpu as pltpu
from jax.sharding import PartitionSpec as P


BF16 = jnp.bfloat16
F32 = jnp.float32
TOK, WIDTH, EXPERTS, CAP, HID = 128, 4096, 16, 20, 128
HALF = WIDTH // 2
ROWS = 2 * EXPERTS * CAP
STEPS = 1
COLS = HALF // STEPS
BLOCKS = WIDTH // 128


def half_of_row(shape, axis):
    row = lax.broadcasted_iota(jnp.int32, shape, axis)
    group = (row * 1639) >> 16
    rest = row - group * (2 * CAP)
    upper = rest >= CAP
    return upper, group * CAP + jnp.where(upper, rest - CAP, rest)


def targets(ids):
    expert = lax.broadcasted_iota(jnp.int32, (EXPERTS, TOK), 0)
    first = (jnp.broadcast_to(ids[0:1, :], (EXPERTS, TOK)) == expert).astype(F32)
    second = (jnp.broadcast_to(ids[1:2, :], (EXPERTS, TOK)) == expert).astype(F32)
    earlier = lax.broadcasted_iota(jnp.int32, (TOK, TOK), 0) < lax.broadcasted_iota(
        jnp.int32, (TOK, TOK), 1
    )
    before = jnp.dot(
        (first + second).astype(BF16),
        earlier.astype(F32).astype(BF16),
        preferred_element_type=F32,
    )
    rank0 = jnp.sum(first * before, 0, keepdims=True).astype(jnp.int32)
    rank1 = jnp.sum(second * before, 0, keepdims=True).astype(jnp.int32)
    return ids[0:1, :] * CAP + rank0, ids[1:2, :] * CAP + rank1


def hits(ids):
    target0, target1 = targets(ids)
    upper, slot = half_of_row((ROWS, TOK), 0)
    hit0 = slot == jnp.broadcast_to(target0, (ROWS, TOK))
    hit1 = slot == jnp.broadcast_to(target1, (ROWS, TOK))
    return hit0, hit1, upper


def placement(hit0, hit1, upper):
    hit = jnp.where(hit0 | hit1, 1.0, 0.0)
    return jnp.concatenate([jnp.where(upper, 0.0, hit), jnp.where(upper, hit, 0.0)], 1)


def place_kernel(
    ids_ref, gates_ref, x_low_ref, x_high_ref, dy_low_ref, dy_high_ref, out_ref, place, gate
):
    step = pl.program_id(0)

    @pl.when(step == 0)
    def _():
        place[...] = placement(*hits(ids_ref[...])).astype(BF16)

    @pl.when(step < STEPS)
    def _():
        both = jnp.concatenate([x_low_ref[...], x_high_ref[...]], 0)
        out_ref[...] = jnp.dot(place[...], both, preferred_element_type=F32).astype(BF16)

    @pl.when(step == STEPS)
    def _():
        hit0, hit1, _ = hits(ids_ref[...])
        gates = gates_ref[...]
        weight = jnp.where(hit0, jnp.broadcast_to(gates[0:1, :], (ROWS, TOK)), 0.0) + jnp.where(
            hit1, jnp.broadcast_to(gates[1:2, :], (ROWS, TOK)), 0.0
        )
        gate[...] = jnp.broadcast_to(jnp.sum(weight, 1, keepdims=True), (ROWS, 128))

    @pl.when(step >= STEPS)
    def _():
        both = jnp.concatenate([dy_low_ref[...], dy_high_ref[...]], 0)
        picked = jnp.dot(place[...], both, preferred_element_type=F32)
        scale = gate[...]
        for i in range(COLS // 128):
            part = picked[:, i * 128 : i * 128 + 128] * scale
            out_ref[:, i * 128 : i * 128 + 128] = part.astype(BF16)


def back_kernel(ids_ref, back_ref):
    back_ref[...] = placement(*hits(ids_ref[...])).T.astype(BF16)


def join_halves(acc, width):
    upper, _ = half_of_row((ROWS, width), 0)
    own = jnp.where(upper, acc[:, width:], acc[:, :width])
    other = jnp.where(upper, pltpu.roll(own, CAP, 0), pltpu.roll(own, ROWS - CAP, 0))
    return own + other


def stack_rows(table_ref, weights, step, h, start, stop):
    count = COLS // 128
    first = count * step + BLOCKS // 2 * h
    return jnp.concatenate(
        [weights[table_ref[first + j], :, start:stop] for j in range(count)], 0
    )


def piece_copies(pieces, weights, sems):
    copies, at = [], 0
    for i, piece in enumerate(pieces):
        span = piece.shape[0]
        copies.append(pltpu.make_async_copy(piece, weights.at[pl.ds(at, span)], sems.at[i]))
        at += span
    return copies


def column_copy(recv_ref, slots, sems, i):
    at = pl.ds(pl.multiple_of(i * COLS, COLS), COLS)
    return pltpu.make_async_copy(recv_ref.at[:, at], slots.at[:, at], sems.at[i])


def expert_kernel(table_ref, info_ref, recv_ref, *refs):
    gathered, both_ref, pieces = refs[:5], refs[5], refs[6:11]
    slots, weights, turned_ref, gate_up, down, sems, w_sems = refs[11:]
    step = pl.program_id(0)

    @pl.when(step == 0)
    def _():
        copies = piece_copies(gathered, weights, w_sems)
        for copy in copies:
            copy.start()
        for i in range(2 * STEPS):
            column_copy(recv_ref, slots, sems, i).start()
        gate_up[...] = jnp.zeros_like(gate_up)
        down[...] = jnp.zeros_like(down)
        for copy in copies:
            copy.wait()

    @pl.when(step < 2 * STEPS)
    def _():
        column_copy(recv_ref, slots, sems, step).wait()

    @pl.when(step < STEPS)
    def _():
        x = slots[:, pl.ds(pl.multiple_of(step * COLS, COLS), COLS)]
        for h in range(2):
            gate_up[:, 2 * HID * h : 2 * HID * (h + 1)] += jnp.dot(
                x,
                stack_rows(table_ref, weights, step, h, 0, 2 * HID),
                preferred_element_type=F32,
            )

    @pl.when((step >= STEPS) & (step < 2 * STEPS))
    def _():
        dy = slots[:, pl.ds(pl.multiple_of(step * COLS, COLS), COLS)]
        w_down = [
            stack_rows(table_ref, weights, step - STEPS, h, 2 * HID, 3 * HID) for h in range(2)
        ]
        down[...] += jnp.dot(dy, jnp.concatenate(w_down, 1), preferred_element_type=F32)

    @pl.when(step == 2 * STEPS - 1)
    def _():
        joined = join_halves(gate_up[...], 2 * HID)
        hid_grad = join_halves(down[...], HID)
        gate_pre = joined[:, :HID]
        up_pre = joined[:, HID:]
        sigmoid_g = jax.nn.sigmoid(gate_pre)
        silu_val = gate_pre * sigmoid_g
        silu_slope = sigmoid_g * (1.0 + gate_pre * (1.0 - sigmoid_g))
        gate_grad = hid_grad * up_pre * silu_slope
        up_grad = hid_grad * silu_val
        hidden = silu_val * up_pre
        both_ref[:, :HID] = gate_grad.astype(BF16)
        both_ref[:, HID:] = up_grad.astype(BF16)
        upper, _ = half_of_row((HID, ROWS), 1)
        for i, value in enumerate((gate_grad, up_grad, hidden)):
            turned = value.T
            turned_ref[i * HID : (i + 1) * HID, :] = jnp.where(upper, 0.0, turned).astype(BF16)
            turned_ref[(i + 3) * HID : (i + 4) * HID, :] = jnp.where(upper, turned, 0.0).astype(
                BF16
            )

    @pl.when(step >= 2 * STEPS)
    def _():
        weight_grad(info_ref, step - 2 * STEPS, slots, turned_ref, pieces)


def weight_grad(info_ref, step, slots, turned_ref, pieces):
    at = pl.multiple_of(step * COLS, COLS)
    x = slots[:, pl.ds(at, COLS)]
    dy = slots[:, pl.ds(pl.multiple_of(at + HALF, COLS), COLS)]
    spans = tuple(zip(pieces, (0, 7, 15, 17, 24), (7, 15, 17, 24, 32)))
    for h in range(2):
        base = 3 * HID * h
        proj = jnp.dot(turned_ref[base : base + 2 * HID, :], x, preferred_element_type=F32)
        down = jnp.dot(
            turned_ref[base + 2 * HID : base + 3 * HID, :], dy, preferred_element_type=F32
        )
        for i in range(COLS // 128):
            block = step * (COLS // 128) + i + h * (BLOCKS // 2)
            keep = info_ref[block].astype(F32)
            place = info_ref[BLOCKS + block]
            top = (proj[:, i * 128 : i * 128 + 128] * keep).astype(BF16)
            bottom = (down[:, i * 128 : i * 128 + 128] * keep).astype(BF16)

            def put(ref, first):
                ref[place - first, : 2 * HID, :] = top
                ref[place - first, 2 * HID :, :] = bottom

            for ref, first, last in spans:
                pl.when((place >= first) & (place < last))(functools.partial(put, ref, first))


def slot_grad_kernel(table_ref, both_ref, *refs):
    gathered, (out_ref, weights, w_sems) = refs[:5], refs[5:]
    step = pl.program_id(0)

    @pl.when(step == 0)
    def _():
        copies = piece_copies(gathered, weights, w_sems)
        for copy in copies:
            copy.start()
        for copy in copies:
            copy.wait()

    both = both_ref[...]
    upper, _ = half_of_row((ROWS, 2 * HID), 0)
    zero = jnp.zeros_like(both)
    total = None
    for h in range(2):
        own = jnp.where(upper, both, zero) if h else jnp.where(upper, zero, both)
        part = lax.dot_general(
            own,
            stack_rows(table_ref, weights, step, h, 0, 2 * HID),
            (((1,), (1,)), ((), ())),
            preferred_element_type=F32,
        )
        total = part if total is None else total + part
    out_ref[...] = total.astype(BF16)


def combine_kernel(back_ref, slots_ref, out_ref):
    step = pl.program_id(0)
    total = jnp.dot(back_ref[...], slots_ref[...], preferred_element_type=F32).astype(BF16)
    at = pl.multiple_of(step * COLS, COLS)
    out_ref[:, pl.ds(at, COLS)] = total[:TOK, :]
    out_ref[:, pl.ds(pl.multiple_of(at + HALF, COLS), COLS)] = total[TOK:, :]


def whole(shape):
    return pl.BlockSpec(shape, lambda i, *_: (0,) * len(shape))


def columns(rows, at=lambda i: i):
    return pl.BlockSpec((rows, COLS), lambda i, *_: (0, at(i)))


def call(kernel, steps, ins, outs, shapes, flops, nbytes, scratch=(), prefetch=0):
    return pl.pallas_call(
        kernel,
        grid_spec=pltpu.PrefetchScalarGridSpec(
            num_scalar_prefetch=prefetch,
            grid=(steps,),
            in_specs=ins,
            out_specs=outs,
            scratch_shapes=list(scratch),
        ),
        out_shape=shapes,
        compiler_params=pltpu.CompilerParams(dimension_semantics=("arbitrary",)),
        cost_estimate=pl.CostEstimate(flops=flops, bytes_accessed=nbytes, transcendentals=0),
    )


def sds(shape, dtype):
    return jax.ShapeDtypeStruct(shape, dtype)


def exchange(rows):
    return lax.all_to_all(
        rows.reshape(EXPERTS, 2 * CAP, -1), "exp", split_axis=0, concat_axis=0, tiled=True
    ).reshape(rows.shape)


def hop(value, distance):
    reps = lax.axis_size("rep")
    turn = [
        (i, (i + 2 * distance) % reps if i % 2 == 0 else (i - 2 * distance) % reps)
        for i in range(reps)
    ]
    return lax.ppermute(value, "rep", turn)


def swap(value):
    return lax.ppermute(value, "rep", [(i, i ^ 1) for i in range(lax.axis_size("rep"))])


def places(rep, sign):
    block = jnp.arange(BLOCKS, dtype=jnp.int32)
    core = rep & 1
    kind = block & 1
    ahead = (sign * ((block >> 1) - (rep >> 1))) & 15
    carrier = jnp.where(ahead == 8, kind, (ahead > 8).astype(jnp.int32))
    carrier = jnp.where(ahead == 0, core, carrier)
    distance = jnp.where(ahead > 8, 16 - ahead, ahead)
    odd = (distance & 1) == 1
    step = jnp.where(odd, distance, distance - 1)
    second = (kind != carrier).astype(jnp.int32)
    pair = 2 * ((step & 2) + ((step >> 2) & 1)) + second
    return distance == 0, odd, pair, second, carrier == core


def gathered_places(rep):
    here, odd, pair, second, local = places(rep, -1)
    at = jnp.where(here, second, jnp.where(odd, 2, 10) + pair)
    return jnp.where(local, at, at + 16)


def scattered_places(rep):
    here, odd, pair, second, local = places(rep, 1)
    at = jnp.where(here, 15 + second, jnp.where(odd, 7, 0) + pair)
    return jnp.where(local, at, at + 17)


def gather_weights(own):
    near = jnp.stack([own, swap(own)])
    one = hop(near, 1)
    five = hop(one, 4)
    three_seven = hop(jnp.concatenate([one, five]), 2)
    odd = jnp.concatenate([one, five, three_seven])
    even = hop(odd, 1)
    return near, odd, even, swap(odd), swap(even)


def scatter_sum(even, odd, give_odd):
    def add(*parts):
        return functools.reduce(jnp.add, [part.astype(F32) for part in parts])

    one = hop(even, 1)
    got = swap(give_odd)
    last = lax.pad(one, jnp.zeros((), BF16), ((-4, 1, 0), (0, 0, 0), (0, 0, 0)))
    second = add(odd[4:], got[4:], last).astype(BF16)
    two = hop(second, 2)
    four = hop(add(odd[2:4], got[2:4], one[2:4], two[2:]).astype(BF16), 4)
    return hop(add(odd[:2], got[:2], one[:2], two[:2], four).astype(BF16), 1)


def per_device(tokens, grad_out, gates, expert_ids, w_all, touched):
    rep = lax.axis_index("rep")
    ids = expert_ids.T
    mbytes = 1 << 20
    early = lambda i: jnp.minimum(i, STEPS - 1)
    late = lambda i: jnp.maximum(i - STEPS, 0)
    sent = call(
        place_kernel,
        2 * STEPS,
        [
            whole((2, TOK)),
            whole((2, TOK)),
            columns(TOK, early),
            columns(TOK, lambda i: early(i) + STEPS),
            columns(TOK, late),
            columns(TOK, lambda i: late(i) + STEPS),
        ],
        columns(ROWS),
        sds((ROWS, WIDTH), BF16),
        4 * ROWS * 256 * HALF,
        8 * mbytes,
        [pltpu.VMEM((ROWS, 2 * TOK), BF16), pltpu.VMEM((ROWS, 128), F32)],
    )(ids, gates.T, tokens, tokens, grad_out, grad_out)
    received = exchange(sent)
    back = call(
        back_kernel,
        1,
        [whole((2, TOK))],
        whole((2 * TOK, ROWS)),
        sds((2 * TOK, ROWS), BF16),
        0,
        mbytes,
    )(ids)
    gathered = gather_weights(w_all[0])
    in_place = [pl.BlockSpec(memory_space=pl.ANY)]
    weights = [
        pltpu.VMEM((sum(piece.shape[0] for piece in gathered), 128, 3 * HID), BF16),
        pltpu.SemaphoreType.DMA((len(gathered),)),
    ]
    table = gathered_places(rep)
    info = jnp.concatenate([touched.reshape(-1), scattered_places(rep)])
    shares = [(n, 3 * HID, 128) for n in (7, 8, 2, 7, 8)]
    both_grad, even, odd, here, give_even, give_odd = call(
        expert_kernel,
        3 * STEPS,
        in_place * 6,
        [whole((ROWS, 2 * HID))] + [whole(share) for share in shares],
        [sds((ROWS, 2 * HID), BF16)] + [sds(share, BF16) for share in shares],
        2 * ROWS * HALF * 12 * HID,
        16 * mbytes,
        [
            pltpu.VMEM((ROWS, WIDTH), BF16),
            weights[0],
            pltpu.VMEM((6 * HID, ROWS), BF16),
            pltpu.VMEM((ROWS, 4 * HID), F32),
            pltpu.VMEM((ROWS, 2 * HID), F32),
            pltpu.SemaphoreType.DMA((2 * STEPS,)),
            weights[1],
        ],
        2,
    )(table, info, received, *gathered)
    paired = (even.astype(F32) + swap(give_even).astype(F32)).astype(BF16)
    paired, both_grad = lax.optimization_barrier((paired, both_grad))
    final = scatter_sum(paired, odd, give_odd)
    slot_grad = call(
        slot_grad_kernel,
        STEPS,
        [whole((ROWS, 2 * HID))] + in_place * 5,
        columns(ROWS),
        sds((ROWS, HALF), BF16),
        2 * ROWS * HALF * 4 * HID,
        6 * mbytes,
        weights,
        1,
    )(table, both_grad, *gathered)
    returned = exchange(slot_grad)
    token_grad = call(
        combine_kernel,
        STEPS,
        [whole((2 * TOK, ROWS)), columns(ROWS)],
        whole((TOK, WIDTH)),
        sds((TOK, WIDTH), BF16),
        2 * ROWS * 256 * HALF,
        4 * mbytes,
    )(back, returned)
    final, token_grad = lax.optimization_barrier((final, token_grad))
    total = here.astype(F32) + final.astype(F32)
    owned = total[:1] + swap(total[1:].astype(BF16)).astype(F32)
    return (token_grad, jnp.swapaxes(owned, 1, 2))


def solution(mesh):
    in_specs = (
        P(("rep", "exp"), None),
        P(("rep", "exp"), None),
        P(("rep", "exp"), None),
        P(("rep", "exp"), None),
        P("exp", "rep", None),
        P("rep", "exp", None),
    )
    out_specs = (P(("rep", "exp"), None), P("exp", "rep", None))

    return jax.shard_map(
        per_device, mesh=mesh, in_specs=in_specs, out_specs=out_specs, check_vma=False
    )
```

```python
import functools

import jax
import jax.numpy as jnp
from jax import lax
from jax.experimental import pallas as pl
from jax.experimental.pallas import tpu as pltpu
from jax.sharding import PartitionSpec as P


BF16 = jnp.bfloat16
F32 = jnp.float32
TOK, WIDTH, EXPERTS, CAP, HID = 128, 4096, 16, 20, 128
HALF = WIDTH // 2
ROWS = 2 * EXPERTS * CAP
STEPS = 1
PARTS = 2
COLS = HALF // STEPS
BLOCKS = WIDTH // 128


def half_of_row(shape, axis):
    row = lax.broadcasted_iota(jnp.int32, shape, axis)
    group = (row * 1639) >> 16
    rest = row - group * (2 * CAP)
    upper = rest >= CAP
    return upper, group * CAP + jnp.where(upper, rest - CAP, rest)


def targets(ids):
    expert = lax.broadcasted_iota(jnp.int32, (EXPERTS, TOK), 0)
    first = (jnp.broadcast_to(ids[0:1, :], (EXPERTS, TOK)) == expert).astype(F32)
    second = (jnp.broadcast_to(ids[1:2, :], (EXPERTS, TOK)) == expert).astype(F32)
    earlier = lax.broadcasted_iota(jnp.int32, (TOK, TOK), 0) < lax.broadcasted_iota(
        jnp.int32, (TOK, TOK), 1
    )
    before = jnp.dot(
        (first + second).astype(BF16),
        earlier.astype(F32).astype(BF16),
        preferred_element_type=F32,
    )
    rank0 = jnp.sum(first * before, 0, keepdims=True).astype(jnp.int32)
    rank1 = jnp.sum(second * before, 0, keepdims=True).astype(jnp.int32)
    return ids[0:1, :] * CAP + rank0, ids[1:2, :] * CAP + rank1


def hits(ids):
    target0, target1 = targets(ids)
    upper, slot = half_of_row((ROWS, TOK), 0)
    hit0 = slot == jnp.broadcast_to(target0, (ROWS, TOK))
    hit1 = slot == jnp.broadcast_to(target1, (ROWS, TOK))
    return hit0, hit1, upper


def placement(hit0, hit1, upper):
    hit = jnp.where(hit0 | hit1, 1.0, 0.0)
    return jnp.concatenate([jnp.where(upper, 0.0, hit), jnp.where(upper, hit, 0.0)], 1)


def place_kernel(
    ids_ref, gates_ref, x_low_ref, x_high_ref, dy_low_ref, dy_high_ref, out_ref, place, gate
):
    step = pl.program_id(0)

    @pl.when(step == 0)
    def _():
        place[...] = placement(*hits(ids_ref[...])).astype(BF16)

    @pl.when(step < STEPS)
    def _():
        both = jnp.concatenate([x_low_ref[...], x_high_ref[...]], 0)
        out_ref[...] = jnp.dot(place[...], both, preferred_element_type=F32).astype(BF16)

    @pl.when(step == STEPS)
    def _():
        hit0, hit1, _ = hits(ids_ref[...])
        gates = gates_ref[...]
        weight = jnp.where(hit0, jnp.broadcast_to(gates[0:1, :], (ROWS, TOK)), 0.0) + jnp.where(
            hit1, jnp.broadcast_to(gates[1:2, :], (ROWS, TOK)), 0.0
        )
        gate[...] = jnp.broadcast_to(jnp.sum(weight, 1, keepdims=True), (ROWS, 128))

    @pl.when(step >= STEPS)
    def _():
        both = jnp.concatenate([dy_low_ref[...], dy_high_ref[...]], 0)
        picked = jnp.dot(place[...], both, preferred_element_type=F32)
        scale = gate[...]
        for i in range(COLS // 128):
            part = picked[:, i * 128 : i * 128 + 128] * scale
            out_ref[:, i * 128 : i * 128 + 128] = part.astype(BF16)


def back_kernel(ids_ref, back_ref):
    back_ref[...] = placement(*hits(ids_ref[...])).T.astype(BF16)


def join_halves(low, high):
    upper, _ = half_of_row(low.shape, 0)
    own = jnp.where(upper, high, low)
    other = jnp.where(upper, pltpu.roll(own, CAP, 0), pltpu.roll(own, ROWS - CAP, 0))
    return own + other


def stack_rows(table_ref, weights, step, h, start, stop):
    count = COLS // 128
    first = count * step + BLOCKS // 2 * h
    return jnp.concatenate(
        [weights[table_ref[first + j], :, start:stop] for j in range(count)], 0
    )


def piece_copies(pieces, weights, sems):
    copies, at = [], 0
    for i, piece in enumerate(pieces):
        span = piece.shape[0]
        copies.append(pltpu.make_async_copy(piece, weights.at[pl.ds(at, span)], sems.at[i]))
        at += span
    return copies


def expert_kernel(table_ref, info_ref, recv_ref, *refs):
    gathered, both_ref, pieces = refs[:5], refs[5], refs[6:11]
    slots, weights, turned_ref, staged, sems, w_sems, out_sems = refs[11:]
    w_copies = piece_copies(gathered, weights, w_sems)
    for copy in w_copies:
        copy.start()
    halves = []
    for i in range(2):
        at = pl.ds(i * HALF, HALF)
        halves.append(pltpu.make_async_copy(recv_ref.at[:, at], slots.at[:, at], sems.at[i]))
        halves[-1].start()
    for copy in w_copies:
        copy.wait()
    halves[0].wait()
    x = slots[:, :HALF]
    gate_up = [
        jnp.dot(x, stack_rows(table_ref, weights, 0, h, 0, 2 * HID), preferred_element_type=F32)
        for h in range(2)
    ]
    joined = join_halves(*gate_up)
    gate_pre = joined[:, :HID]
    up_pre = joined[:, HID:]
    sigmoid_g = jax.nn.sigmoid(gate_pre)
    silu_val = gate_pre * sigmoid_g
    silu_slope = sigmoid_g * (1.0 + gate_pre * (1.0 - sigmoid_g))
    hidden = silu_val * up_pre
    halves[1].wait()
    dy = slots[:, HALF:]
    w_down = [stack_rows(table_ref, weights, 0, h, 2 * HID, 3 * HID) for h in range(2)]
    down = jnp.dot(dy, jnp.concatenate(w_down, 1), preferred_element_type=F32)
    hid_grad = join_halves(down[:, :HID], down[:, HID:])
    gate_grad = hid_grad * up_pre * silu_slope
    up_grad = hid_grad * silu_val
    both_ref[:, :HID] = gate_grad.astype(BF16)
    both_ref[:, HID:] = up_grad.astype(BF16)
    upper, _ = half_of_row((HID, ROWS), 1)
    for i, value in enumerate((gate_grad, up_grad, hidden)):
        turned = value.T
        turned_ref[i * HID : (i + 1) * HID, :] = jnp.where(upper, 0.0, turned).astype(BF16)
        turned_ref[(i + 3) * HID : (i + 4) * HID, :] = jnp.where(upper, turned, 0.0).astype(BF16)
    spans = tuple(zip(pieces, (0, 7, 15, 17, 24), (7, 15, 17, 24, 32)))
    for part in range(PARTS):
        columns_of = slice(part * HALF // PARTS, (part + 1) * HALF // PARTS)
        for h in range(2):
            base = 3 * HID * h
            proj = jnp.dot(
                turned_ref[base : base + 2 * HID, :],
                slots[:, columns_of],
                preferred_element_type=F32,
            )
            down = jnp.dot(
                turned_ref[base + 2 * HID : base + 3 * HID, :],
                slots[:, HALF + columns_of.start : HALF + columns_of.stop],
                preferred_element_type=F32,
            )
            for i in range(HALF // PARTS // 128):
                block = columns_of.start // 128 + i + h * (BLOCKS // 2)
                keep = info_ref[block].astype(F32)
                place = info_ref[BLOCKS + block]
                lanes = slice(i * 128, i * 128 + 128)
                staged[block, : 2 * HID, :] = (proj[:, lanes] * keep).astype(BF16)
                staged[block, 2 * HID :, :] = (down[:, lanes] * keep).astype(BF16)

                def send(ref, first):
                    pltpu.make_async_copy(
                        staged.at[block], ref.at[place - first], out_sems.at[block]
                    ).start()

                for ref, first, last in spans:
                    pl.when((place >= first) & (place < last))(
                        functools.partial(send, ref, first)
                    )
    for block in range(BLOCKS):
        pltpu.make_async_copy(staged.at[block], pieces[0].at[0], out_sems.at[block]).wait()


def slot_grad_kernel(table_ref, both_ref, *refs):
    gathered, (out_ref, weights, w_sems) = refs[:5], refs[5:]
    step = pl.program_id(0)

    @pl.when(step == 0)
    def _():
        copies = piece_copies(gathered, weights, w_sems)
        for copy in copies:
            copy.start()
        for copy in copies:
            copy.wait()

    both = both_ref[...]
    upper, _ = half_of_row((ROWS, 2 * HID), 0)
    zero = jnp.zeros_like(both)
    total = None
    for h in range(2):
        own = jnp.where(upper, both, zero) if h else jnp.where(upper, zero, both)
        part = lax.dot_general(
            own,
            stack_rows(table_ref, weights, step, h, 0, 2 * HID),
            (((1,), (1,)), ((), ())),
            preferred_element_type=F32,
        )
        total = part if total is None else total + part
    out_ref[...] = total.astype(BF16)


def combine_kernel(back_ref, slots_ref, out_ref):
    step = pl.program_id(0)
    total = jnp.dot(back_ref[...], slots_ref[...], preferred_element_type=F32).astype(BF16)
    at = pl.multiple_of(step * COLS, COLS)
    out_ref[:, pl.ds(at, COLS)] = total[:TOK, :]
    out_ref[:, pl.ds(pl.multiple_of(at + HALF, COLS), COLS)] = total[TOK:, :]


def whole(shape):
    return pl.BlockSpec(shape, lambda i, *_: (0,) * len(shape))


def columns(rows, at=lambda i: i):
    return pl.BlockSpec((rows, COLS), lambda i, *_: (0, at(i)))


def call(kernel, steps, ins, outs, shapes, flops, nbytes, scratch=(), prefetch=0):
    return pl.pallas_call(
        kernel,
        grid_spec=pltpu.PrefetchScalarGridSpec(
            num_scalar_prefetch=prefetch,
            grid=(steps,),
            in_specs=ins,
            out_specs=outs,
            scratch_shapes=list(scratch),
        ),
        out_shape=shapes,
        compiler_params=pltpu.CompilerParams(dimension_semantics=("arbitrary",)),
        cost_estimate=pl.CostEstimate(flops=flops, bytes_accessed=nbytes, transcendentals=0),
    )


def sds(shape, dtype):
    return jax.ShapeDtypeStruct(shape, dtype)


def exchange(rows):
    return lax.all_to_all(
        rows.reshape(EXPERTS, 2 * CAP, -1), "exp", split_axis=0, concat_axis=0, tiled=True
    ).reshape(rows.shape)


def hop(value, distance):
    reps = lax.axis_size("rep")
    turn = [
        (i, (i + 2 * distance) % reps if i % 2 == 0 else (i - 2 * distance) % reps)
        for i in range(reps)
    ]
    return lax.ppermute(value, "rep", turn)


def swap(value):
    return lax.ppermute(value, "rep", [(i, i ^ 1) for i in range(lax.axis_size("rep"))])


def places(rep, sign):
    block = jnp.arange(BLOCKS, dtype=jnp.int32)
    core = rep & 1
    kind = block & 1
    ahead = (sign * ((block >> 1) - (rep >> 1))) & 15
    carrier = jnp.where(ahead == 8, kind, (ahead > 8).astype(jnp.int32))
    carrier = jnp.where(ahead == 0, core, carrier)
    distance = jnp.where(ahead > 8, 16 - ahead, ahead)
    odd = (distance & 1) == 1
    step = jnp.where(odd, distance, distance - 1)
    second = (kind != carrier).astype(jnp.int32)
    pair = 2 * ((step & 2) + ((step >> 2) & 1)) + second
    return distance == 0, odd, pair, second, carrier == core


def gathered_places(rep):
    here, odd, pair, second, local = places(rep, -1)
    at = jnp.where(here, second, jnp.where(odd, 2, 10) + pair)
    return jnp.where(local, at, at + 16)


def scattered_places(rep):
    here, odd, pair, second, local = places(rep, 1)
    at = jnp.where(here, 15 + second, jnp.where(odd, 7, 0) + pair)
    return jnp.where(local, at, at + 17)


def gather_weights(own):
    near = jnp.stack([own, swap(own)])
    one = hop(near, 1)
    five = hop(one, 4)
    three_seven = hop(jnp.concatenate([one, five]), 2)
    odd = jnp.concatenate([one, five, three_seven])
    even = hop(odd, 1)
    return near, odd, even, swap(odd), swap(even)


def add(*parts):
    return functools.reduce(jnp.add, [part.astype(F32) for part in parts])


def scatter_sum(even, odd, give_odd):
    one = hop(even, 1)
    got = swap(give_odd)
    last = lax.pad(one, jnp.zeros((), BF16), ((-4, 1, 0), (0, 0, 0), (0, 0, 0)))
    second = add(odd[4:], got[4:], last).astype(BF16)
    two = hop(second, 2)
    five = hop(add(odd[2:4], got[2:4], one[2:4], two[2:]).astype(BF16), 5)
    return five, hop(add(odd[:2], got[:2], one[:2], two[:2]).astype(BF16), 1)


def per_device(tokens, grad_out, gates, expert_ids, w_all, touched):
    rep = lax.axis_index("rep")
    ids = expert_ids.T
    mbytes = 1 << 20
    early = lambda i: jnp.minimum(i, STEPS - 1)
    late = lambda i: jnp.maximum(i - STEPS, 0)
    sent = call(
        place_kernel,
        2 * STEPS,
        [
            whole((2, TOK)),
            whole((2, TOK)),
            columns(TOK, early),
            columns(TOK, lambda i: early(i) + STEPS),
            columns(TOK, late),
            columns(TOK, lambda i: late(i) + STEPS),
        ],
        columns(ROWS),
        sds((ROWS, WIDTH), BF16),
        4 * ROWS * 256 * HALF,
        8 * mbytes,
        [pltpu.VMEM((ROWS, 2 * TOK), BF16), pltpu.VMEM((ROWS, 128), F32)],
    )(ids, gates.T, tokens, tokens, grad_out, grad_out)
    received = exchange(sent)
    back = call(
        back_kernel,
        1,
        [whole((2, TOK))],
        whole((2 * TOK, ROWS)),
        sds((2 * TOK, ROWS), BF16),
        0,
        mbytes,
    )(ids)
    gathered = gather_weights(w_all[0])
    in_place = [pl.BlockSpec(memory_space=pl.ANY)]
    weights = [
        pltpu.VMEM((sum(piece.shape[0] for piece in gathered), 128, 3 * HID), BF16),
        pltpu.SemaphoreType.DMA((len(gathered),)),
    ]
    table = gathered_places(rep)
    info = jnp.concatenate([touched.reshape(-1), scattered_places(rep)])
    shares = [(n, 3 * HID, 128) for n in (7, 8, 2, 7, 8)]
    both_grad, even, odd, here, give_even, give_odd = call(
        expert_kernel,
        1,
        in_place * 6,
        [whole((ROWS, 2 * HID))] + in_place * 5,
        [sds((ROWS, 2 * HID), BF16)] + [sds(share, BF16) for share in shares],
        2 * ROWS * HALF * 12 * HID,
        16 * mbytes,
        [
            pltpu.VMEM((ROWS, WIDTH), BF16),
            weights[0],
            pltpu.VMEM((6 * HID, ROWS), BF16),
            pltpu.VMEM((BLOCKS, 3 * HID, 128), BF16),
            pltpu.SemaphoreType.DMA((2,)),
            weights[1],
            pltpu.SemaphoreType.DMA((BLOCKS,)),
        ],
        2,
    )(table, info, received, *gathered)
    paired = (even.astype(F32) + swap(give_even).astype(F32)).astype(BF16)
    paired, both_grad = lax.optimization_barrier((paired, both_grad))
    final = scatter_sum(paired, odd, give_odd)
    slot_grad = call(
        slot_grad_kernel,
        STEPS,
        [whole((ROWS, 2 * HID))] + in_place * 5,
        columns(ROWS),
        sds((ROWS, HALF), BF16),
        2 * ROWS * HALF * 4 * HID,
        6 * mbytes,
        weights,
        1,
    )(table, both_grad, *gathered)
    returned = exchange(slot_grad)
    token_grad = call(
        combine_kernel,
        STEPS,
        [whole((2 * TOK, ROWS)), columns(ROWS)],
        whole((TOK, WIDTH)),
        sds((TOK, WIDTH), BF16),
        2 * ROWS * 256 * HALF,
        4 * mbytes,
    )(back, returned)
    final, token_grad = lax.optimization_barrier((final, token_grad))
    total = add(here, *final)
    owned = total[:1] + swap(total[1:].astype(BF16)).astype(F32)
    return (token_grad, jnp.swapaxes(owned, 1, 2))


def solution(mesh):
    in_specs = (
        P(("rep", "exp"), None),
        P(("rep", "exp"), None),
        P(("rep", "exp"), None),
        P(("rep", "exp"), None),
        P("exp", "rep", None),
        P("rep", "exp", None),
    )
    out_specs = (P(("rep", "exp"), None), P("exp", "rep", None))

    return jax.shard_map(
        per_device, mesh=mesh, in_specs=in_specs, out_specs=out_specs, check_vma=False
    )
```

```python
import functools

import jax
import jax.numpy as jnp
from jax import lax
from jax.experimental import pallas as pl
from jax.experimental.pallas import tpu as pltpu
from jax.sharding import PartitionSpec as P


BF16 = jnp.bfloat16
F32 = jnp.float32
TOK, WIDTH, EXPERTS, CAP, HID = 128, 4096, 16, 20, 128
HALF = WIDTH // 2
ROWS = 2 * EXPERTS * CAP
STEPS = 1
PARTS = 2
GRAD_PARTS = 4
COLS = HALF // STEPS
BLOCKS = WIDTH // 128


def half_of_row(shape, axis):
    row = lax.broadcasted_iota(jnp.int32, shape, axis)
    group = (row * 1639) >> 16
    rest = row - group * (2 * CAP)
    upper = rest >= CAP
    return upper, group * CAP + jnp.where(upper, rest - CAP, rest)


def targets(ids):
    expert = lax.broadcasted_iota(jnp.int32, (EXPERTS, TOK), 0)
    first = (jnp.broadcast_to(ids[0:1, :], (EXPERTS, TOK)) == expert).astype(F32)
    second = (jnp.broadcast_to(ids[1:2, :], (EXPERTS, TOK)) == expert).astype(F32)
    earlier = lax.broadcasted_iota(jnp.int32, (TOK, TOK), 0) < lax.broadcasted_iota(
        jnp.int32, (TOK, TOK), 1
    )
    before = jnp.dot(
        (first + second).astype(BF16),
        earlier.astype(F32).astype(BF16),
        preferred_element_type=F32,
    )
    rank0 = jnp.sum(first * before, 0, keepdims=True).astype(jnp.int32)
    rank1 = jnp.sum(second * before, 0, keepdims=True).astype(jnp.int32)
    return ids[0:1, :] * CAP + rank0, ids[1:2, :] * CAP + rank1


def hits(ids):
    target0, target1 = targets(ids)
    upper, slot = half_of_row((ROWS, TOK), 0)
    hit0 = slot == jnp.broadcast_to(target0, (ROWS, TOK))
    hit1 = slot == jnp.broadcast_to(target1, (ROWS, TOK))
    return hit0, hit1, upper


def placement(hit0, hit1, upper):
    hit = jnp.where(hit0 | hit1, 1.0, 0.0)
    return jnp.concatenate([jnp.where(upper, 0.0, hit), jnp.where(upper, hit, 0.0)], 1)


def place_kernel(
    ids_ref, gates_ref, x_low_ref, x_high_ref, dy_low_ref, dy_high_ref, out_ref, place, gate
):
    step = pl.program_id(0)

    @pl.when(step == 0)
    def _():
        place[...] = placement(*hits(ids_ref[...])).astype(BF16)

    @pl.when(step < STEPS)
    def _():
        both = jnp.concatenate([x_low_ref[...], x_high_ref[...]], 0)
        out_ref[...] = jnp.dot(place[...], both, preferred_element_type=F32).astype(BF16)

    @pl.when(step == STEPS)
    def _():
        hit0, hit1, _ = hits(ids_ref[...])
        gates = gates_ref[...]
        weight = jnp.where(hit0, jnp.broadcast_to(gates[0:1, :], (ROWS, TOK)), 0.0) + jnp.where(
            hit1, jnp.broadcast_to(gates[1:2, :], (ROWS, TOK)), 0.0
        )
        gate[...] = jnp.broadcast_to(jnp.sum(weight, 1, keepdims=True), (ROWS, 128))

    @pl.when(step >= STEPS)
    def _():
        both = jnp.concatenate([dy_low_ref[...], dy_high_ref[...]], 0)
        picked = jnp.dot(place[...], both, preferred_element_type=F32)
        scale = gate[...]
        for i in range(COLS // 128):
            part = picked[:, i * 128 : i * 128 + 128] * scale
            out_ref[:, i * 128 : i * 128 + 128] = part.astype(BF16)


def back_kernel(ids_ref, back_ref):
    back_ref[...] = placement(*hits(ids_ref[...])).T.astype(BF16)


def join_halves(low, high):
    upper, _ = half_of_row(low.shape, 0)
    own = jnp.where(upper, high, low)
    other = jnp.where(upper, pltpu.roll(own, CAP, 0), pltpu.roll(own, ROWS - CAP, 0))
    return own + other


def stack_rows(table_ref, weights, first, count, start, stop):
    return jnp.concatenate(
        [weights[table_ref[first + j], :, start:stop] for j in range(count)], 0
    )


def piece_copies(pieces, weights, sems):
    copies, at = [], 0
    for i, piece in enumerate(pieces):
        span = piece.shape[0]
        copies.append(pltpu.make_async_copy(piece, weights.at[pl.ds(at, span)], sems.at[i]))
        at += span
    return copies


def expert_kernel(table_ref, info_ref, recv_ref, *refs):
    gathered, slot_grad_ref, pieces = refs[:5], refs[5], refs[6:11]
    slots, weights, turned_ref, staged, grads, sems, w_sems, out_sems, grad_sems = refs[11:]
    w_copies = piece_copies(gathered, weights, w_sems)
    for copy in w_copies:
        copy.start()
    halves = []
    for i in range(2):
        at = pl.ds(i * HALF, HALF)
        halves.append(pltpu.make_async_copy(recv_ref.at[:, at], slots.at[:, at], sems.at[i]))
        halves[-1].start()
    for copy in w_copies:
        copy.wait()
    halves[0].wait()
    x = slots[:, :HALF]
    gate_up = [
        jnp.dot(
            x,
            stack_rows(table_ref, weights, BLOCKS // 2 * h, BLOCKS // 2, 0, 2 * HID),
            preferred_element_type=F32,
        )
        for h in range(2)
    ]
    joined = join_halves(*gate_up)
    gate_pre = joined[:, :HID]
    up_pre = joined[:, HID:]
    sigmoid_g = jax.nn.sigmoid(gate_pre)
    silu_val = gate_pre * sigmoid_g
    silu_slope = sigmoid_g * (1.0 + gate_pre * (1.0 - sigmoid_g))
    hidden = silu_val * up_pre
    halves[1].wait()
    dy = slots[:, HALF:]
    w_down = [
        stack_rows(table_ref, weights, BLOCKS // 2 * h, BLOCKS // 2, 2 * HID, 3 * HID)
        for h in range(2)
    ]
    down = jnp.dot(dy, jnp.concatenate(w_down, 1), preferred_element_type=F32)
    hid_grad = join_halves(down[:, :HID], down[:, HID:])
    gate_grad = hid_grad * up_pre * silu_slope
    up_grad = hid_grad * silu_val
    both = jnp.concatenate([gate_grad, up_grad], 1)
    upper, _ = half_of_row(both.shape, 0)
    both = jnp.concatenate([jnp.where(upper, 0.0, both), jnp.where(upper, both, 0.0)], 1)
    both = both.astype(BF16)
    upper, _ = half_of_row((HID, ROWS), 1)
    for i, value in enumerate((gate_grad, up_grad, hidden)):
        turned = value.T
        turned_ref[i * HID : (i + 1) * HID, :] = jnp.where(upper, 0.0, turned).astype(BF16)
        turned_ref[(i + 3) * HID : (i + 4) * HID, :] = jnp.where(upper, turned, 0.0).astype(BF16)
    spans = tuple(zip(pieces, (0, 7, 15, 17, 24), (7, 15, 17, 24, 32)))
    for part in range(PARTS):
        columns_of = slice(part * HALF // PARTS, (part + 1) * HALF // PARTS)
        for h in range(2):
            base = 3 * HID * h
            proj = jnp.dot(
                turned_ref[base : base + 2 * HID, :],
                slots[:, columns_of],
                preferred_element_type=F32,
            )
            down = jnp.dot(
                turned_ref[base + 2 * HID : base + 3 * HID, :],
                slots[:, HALF + columns_of.start : HALF + columns_of.stop],
                preferred_element_type=F32,
            )
            for i in range(HALF // PARTS // 128):
                block = columns_of.start // 128 + i + h * (BLOCKS // 2)
                keep = info_ref[block].astype(F32)
                place = info_ref[BLOCKS + block]
                lanes = slice(i * 128, i * 128 + 128)
                staged[block, : 2 * HID, :] = (proj[:, lanes] * keep).astype(BF16)
                staged[block, 2 * HID :, :] = (down[:, lanes] * keep).astype(BF16)

                def send(ref, first):
                    pltpu.make_async_copy(
                        staged.at[block], ref.at[place - first], out_sems.at[block]
                    ).start()

                for ref, first, last in spans:
                    pl.when((place >= first) & (place < last))(
                        functools.partial(send, ref, first)
                    )
    copies = []
    for part in range(GRAD_PARTS):
        count = BLOCKS // 2 // GRAD_PARTS
        matching = [
            stack_rows(table_ref, weights, count * part + BLOCKS // 2 * h, count, 0, 2 * HID)
            for h in range(2)
        ]
        at = pl.ds(part * count * 128, count * 128)
        grads[:, at] = lax.dot_general(
            both,
            jnp.concatenate(matching, 1),
            (((1,), (1,)), ((), ())),
            preferred_element_type=F32,
        ).astype(BF16)
        copies.append(
            pltpu.make_async_copy(grads.at[:, at], slot_grad_ref.at[:, at], grad_sems.at[part])
        )
        copies[-1].start()
    for copy in copies:
        copy.wait()
    for block in range(BLOCKS):
        pltpu.make_async_copy(staged.at[block], pieces[0].at[0], out_sems.at[block]).wait()


def combine_kernel(back_ref, slots_ref, out_ref):
    step = pl.program_id(0)
    total = jnp.dot(back_ref[...], slots_ref[...], preferred_element_type=F32).astype(BF16)
    at = pl.multiple_of(step * COLS, COLS)
    out_ref[:, pl.ds(at, COLS)] = total[:TOK, :]
    out_ref[:, pl.ds(pl.multiple_of(at + HALF, COLS), COLS)] = total[TOK:, :]


def whole(shape):
    return pl.BlockSpec(shape, lambda i, *_: (0,) * len(shape))


def columns(rows, at=lambda i: i):
    return pl.BlockSpec((rows, COLS), lambda i, *_: (0, at(i)))


def call(kernel, steps, ins, outs, shapes, flops, nbytes, scratch=(), prefetch=0):
    return pl.pallas_call(
        kernel,
        grid_spec=pltpu.PrefetchScalarGridSpec(
            num_scalar_prefetch=prefetch,
            grid=(steps,),
            in_specs=ins,
            out_specs=outs,
            scratch_shapes=list(scratch),
        ),
        out_shape=shapes,
        compiler_params=pltpu.CompilerParams(dimension_semantics=("arbitrary",)),
        cost_estimate=pl.CostEstimate(flops=flops, bytes_accessed=nbytes, transcendentals=0),
    )


def sds(shape, dtype):
    return jax.ShapeDtypeStruct(shape, dtype)


def exchange(rows):
    return lax.all_to_all(
        rows.reshape(EXPERTS, 2 * CAP, -1), "exp", split_axis=0, concat_axis=0, tiled=True
    ).reshape(rows.shape)


def hop(value, distance):
    reps = lax.axis_size("rep")
    turn = [
        (i, (i + 2 * distance) % reps if i % 2 == 0 else (i - 2 * distance) % reps)
        for i in range(reps)
    ]
    return lax.ppermute(value, "rep", turn)


def swap(value):
    return lax.ppermute(value, "rep", [(i, i ^ 1) for i in range(lax.axis_size("rep"))])


def places(rep, sign):
    block = jnp.arange(BLOCKS, dtype=jnp.int32)
    core = rep & 1
    kind = block & 1
    ahead = (sign * ((block >> 1) - (rep >> 1))) & 15
    carrier = jnp.where(ahead == 8, kind, (ahead > 8).astype(jnp.int32))
    carrier = jnp.where(ahead == 0, core, carrier)
    distance = jnp.where(ahead > 8, 16 - ahead, ahead)
    odd = (distance & 1) == 1
    step = jnp.where(odd, distance, distance - 1)
    second = (kind != carrier).astype(jnp.int32)
    pair = 2 * ((step & 2) + ((step >> 2) & 1)) + second
    return distance == 0, odd, pair, second, carrier == core


def gathered_places(rep):
    here, odd, pair, second, local = places(rep, -1)
    at = jnp.where(here, second, jnp.where(odd, 2, 10) + pair)
    return jnp.where(local, at, at + 16)


def scattered_places(rep):
    here, odd, pair, second, local = places(rep, 1)
    at = jnp.where(here, 15 + second, jnp.where(odd, 7, 0) + pair)
    return jnp.where(local, at, at + 17)


def gather_weights(own):
    near = jnp.stack([own, swap(own)])
    one = hop(near, 1)
    five = hop(one, 4)
    three_seven = hop(jnp.concatenate([one, five]), 2)
    odd = jnp.concatenate([one, five, three_seven])
    even = hop(odd, 1)
    return near, odd, even, swap(odd), swap(even)


def add(*parts):
    return functools.reduce(jnp.add, [part.astype(F32) for part in parts])


def scatter_sum(even, odd, give_odd):
    one = hop(even, 1)
    got = swap(give_odd)
    last = lax.pad(one, jnp.zeros((), BF16), ((-4, 1, 0), (0, 0, 0), (0, 0, 0)))
    second = add(odd[4:], got[4:], last).astype(BF16)
    two = hop(second, 2)
    five = hop(add(odd[2:4], got[2:4], one[2:4], two[2:]).astype(BF16), 5)
    return five, hop(add(odd[:2], got[:2], one[:2], two[:2]).astype(BF16), 1)


def per_device(tokens, grad_out, gates, expert_ids, w_all, touched):
    rep = lax.axis_index("rep")
    ids = expert_ids.T
    mbytes = 1 << 20
    early = lambda i: jnp.minimum(i, STEPS - 1)
    late = lambda i: jnp.maximum(i - STEPS, 0)
    sent = call(
        place_kernel,
        2 * STEPS,
        [
            whole((2, TOK)),
            whole((2, TOK)),
            columns(TOK, early),
            columns(TOK, lambda i: early(i) + STEPS),
            columns(TOK, late),
            columns(TOK, lambda i: late(i) + STEPS),
        ],
        columns(ROWS),
        sds((ROWS, WIDTH), BF16),
        4 * ROWS * 256 * HALF,
        8 * mbytes,
        [pltpu.VMEM((ROWS, 2 * TOK), BF16), pltpu.VMEM((ROWS, 128), F32)],
    )(ids, gates.T, tokens, tokens, grad_out, grad_out)
    received = exchange(sent)
    back = call(
        back_kernel,
        1,
        [whole((2, TOK))],
        whole((2 * TOK, ROWS)),
        sds((2 * TOK, ROWS), BF16),
        0,
        mbytes,
    )(ids)
    gathered = gather_weights(w_all[0])
    in_place = [pl.BlockSpec(memory_space=pl.ANY)]
    weights = [
        pltpu.VMEM((sum(piece.shape[0] for piece in gathered), 128, 3 * HID), BF16),
        pltpu.SemaphoreType.DMA((len(gathered),)),
    ]
    table = gathered_places(rep)
    info = jnp.concatenate([touched.reshape(-1), scattered_places(rep)])
    shares = [(n, 3 * HID, 128) for n in (7, 8, 2, 7, 8)]
    slot_grad, even, odd, here, give_even, give_odd = call(
        expert_kernel,
        1,
        in_place * 6,
        in_place * 6,
        [sds((ROWS, HALF), BF16)] + [sds(share, BF16) for share in shares],
        2 * ROWS * HALF * 16 * HID,
        16 * mbytes,
        [
            pltpu.VMEM((ROWS, WIDTH), BF16),
            weights[0],
            pltpu.VMEM((6 * HID, ROWS), BF16),
            pltpu.VMEM((BLOCKS, 3 * HID, 128), BF16),
            pltpu.VMEM((ROWS, HALF), BF16),
            pltpu.SemaphoreType.DMA((2,)),
            weights[1],
            pltpu.SemaphoreType.DMA((BLOCKS,)),
            pltpu.SemaphoreType.DMA((GRAD_PARTS,)),
        ],
        2,
    )(table, info, received, *gathered)
    paired = (even.astype(F32) + swap(give_even).astype(F32)).astype(BF16)
    final = scatter_sum(paired, odd, give_odd)
    returned = exchange(slot_grad)
    token_grad = call(
        combine_kernel,
        STEPS,
        [whole((2 * TOK, ROWS)), columns(ROWS)],
        whole((TOK, WIDTH)),
        sds((TOK, WIDTH), BF16),
        2 * ROWS * 256 * HALF,
        4 * mbytes,
    )(back, returned)
    final, token_grad = lax.optimization_barrier((final, token_grad))
    total = add(here, *final)
    owned = total[:1] + swap(total[1:].astype(BF16)).astype(F32)
    return (token_grad, jnp.swapaxes(owned, 1, 2))


def solution(mesh):
    in_specs = (
        P(("rep", "exp"), None),
        P(("rep", "exp"), None),
        P(("rep", "exp"), None),
        P(("rep", "exp"), None),
        P("exp", "rep", None),
        P("rep", "exp", None),
    )
    out_specs = (P(("rep", "exp"), None), P("exp", "rep", None))

    return jax.shard_map(
        per_device, mesh=mesh, in_specs=in_specs, out_specs=out_specs, check_vma=False
    )
```

```python
import functools

import jax
import jax.numpy as jnp
from jax import lax
from jax.experimental import pallas as pl
from jax.experimental.pallas import tpu as pltpu
from jax.sharding import PartitionSpec as P


BF16 = jnp.bfloat16
F32 = jnp.float32
TOK, WIDTH, EXPERTS, CAP, HID = 128, 4096, 16, 20, 128
HALF = WIDTH // 2
ROWS = 2 * EXPERTS * CAP
STEPS = 2
PARTS = 2
PLACE_PARTS = 4
GRAD_PARTS = 4
COLS = HALF // STEPS
BLOCKS = WIDTH // 128


def half_of_row(shape, axis):
    row = lax.broadcasted_iota(jnp.int32, shape, axis)
    group = (row * 1639) >> 16
    rest = row - group * (2 * CAP)
    upper = rest >= CAP
    return upper, group * CAP + jnp.where(upper, rest - CAP, rest)


def targets(ids):
    expert = lax.broadcasted_iota(jnp.int32, (EXPERTS, TOK), 0)
    first = (jnp.broadcast_to(ids[0:1, :], (EXPERTS, TOK)) == expert).astype(F32)
    second = (jnp.broadcast_to(ids[1:2, :], (EXPERTS, TOK)) == expert).astype(F32)
    earlier = lax.broadcasted_iota(jnp.int32, (TOK, TOK), 0) < lax.broadcasted_iota(
        jnp.int32, (TOK, TOK), 1
    )
    before = jnp.dot(
        (first + second).astype(BF16),
        earlier.astype(F32).astype(BF16),
        preferred_element_type=F32,
    )
    rank0 = jnp.sum(first * before, 0, keepdims=True).astype(jnp.int32)
    rank1 = jnp.sum(second * before, 0, keepdims=True).astype(jnp.int32)
    return ids[0:1, :] * CAP + rank0, ids[1:2, :] * CAP + rank1


def hits(ids):
    target0, target1 = targets(ids)
    upper, slot = half_of_row((ROWS, TOK), 0)
    hit0 = slot == jnp.broadcast_to(target0, (ROWS, TOK))
    hit1 = slot == jnp.broadcast_to(target1, (ROWS, TOK))
    return hit0, hit1, upper


def placement(hit0, hit1, upper):
    hit = jnp.where(hit0 | hit1, 1.0, 0.0)
    return jnp.concatenate([jnp.where(upper, 0.0, hit), jnp.where(upper, hit, 0.0)], 1)


def place_kernel(
    ids_ref, gates_ref, x_ref, dy_ref, out_ref, x, dy, staged, in_sems, out_sems
):
    arrivals = [
        pltpu.make_async_copy(x_ref, x, in_sems.at[0]),
        pltpu.make_async_copy(dy_ref, dy, in_sems.at[1]),
    ]
    for copy in arrivals:
        copy.start()
    hit0, hit1, upper = hits(ids_ref[...])
    place = placement(hit0, hit1, upper).astype(BF16)
    departures = []

    def put(source, at, scale):
        width = HALF // PLACE_PARTS
        for part in range(PLACE_PARTS):
            low = source[:, part * width : (part + 1) * width]
            high = source[:, HALF + part * width : HALF + (part + 1) * width]
            rows = jnp.dot(
                place, jnp.concatenate([low, high], 0), preferred_element_type=F32
            )
            if scale is not None:
                rows = rows * scale
            lanes = pl.ds(at + part * width, width)
            staged[:, lanes] = rows.astype(BF16)
            departures.append(
                pltpu.make_async_copy(
                    staged.at[:, lanes], out_ref.at[:, lanes], out_sems.at[len(departures)]
                )
            )
            departures[-1].start()

    arrivals[0].wait()
    put(x, 0, None)
    gates = gates_ref[...]
    weight = jnp.where(hit0, jnp.broadcast_to(gates[0:1, :], (ROWS, TOK)), 0.0) + jnp.where(
        hit1, jnp.broadcast_to(gates[1:2, :], (ROWS, TOK)), 0.0
    )
    scale = jnp.sum(weight, 1, keepdims=True)
    arrivals[1].wait()
    put(dy, HALF, scale)
    for copy in departures:
        copy.wait()


def back_kernel(ids_ref, back_ref):
    back_ref[...] = placement(*hits(ids_ref[...])).T.astype(BF16)


def join_halves(low, high):
    upper, _ = half_of_row(low.shape, 0)
    own = jnp.where(upper, high, low)
    other = jnp.where(upper, pltpu.roll(own, CAP, 0), pltpu.roll(own, ROWS - CAP, 0))
    return own + other


def stack_rows(table_ref, weights, first, count, start, stop):
    return jnp.concatenate(
        [weights[table_ref[first + j], :, start:stop] for j in range(count)], 0
    )


def piece_copies(pieces, weights, sems):
    copies, at = [], 0
    for i, piece in enumerate(pieces):
        span = piece.shape[0]
        copies.append(pltpu.make_async_copy(piece, weights.at[pl.ds(at, span)], sems.at[i]))
        at += span
    return copies


def expert_kernel(table_ref, info_ref, recv_ref, *refs):
    gathered, slot_grad_ref, pieces = refs[:5], refs[5], refs[6:11]
    slots, weights, turned_ref, staged, grads, sems, w_sems, out_sems, grad_sems = refs[11:]
    w_copies = piece_copies(gathered, weights, w_sems)
    for copy in w_copies:
        copy.start()
    halves = []
    for i in range(2):
        at = pl.ds(i * HALF, HALF)
        halves.append(pltpu.make_async_copy(recv_ref.at[:, at], slots.at[:, at], sems.at[i]))
        halves[-1].start()
    for copy in w_copies:
        copy.wait()
    halves[0].wait()
    x = slots[:, :HALF]
    gate_up = [
        jnp.dot(
            x,
            stack_rows(table_ref, weights, BLOCKS // 2 * h, BLOCKS // 2, 0, 2 * HID),
            preferred_element_type=F32,
        )
        for h in range(2)
    ]
    joined = join_halves(*gate_up)
    gate_pre = joined[:, :HID]
    up_pre = joined[:, HID:]
    sigmoid_g = jax.nn.sigmoid(gate_pre)
    silu_val = gate_pre * sigmoid_g
    silu_slope = sigmoid_g * (1.0 + gate_pre * (1.0 - sigmoid_g))
    hidden = silu_val * up_pre
    halves[1].wait()
    dy = slots[:, HALF:]
    w_down = [
        stack_rows(table_ref, weights, BLOCKS // 2 * h, BLOCKS // 2, 2 * HID, 3 * HID)
        for h in range(2)
    ]
    down = jnp.dot(dy, jnp.concatenate(w_down, 1), preferred_element_type=F32)
    hid_grad = join_halves(down[:, :HID], down[:, HID:])
    gate_grad = hid_grad * up_pre * silu_slope
    up_grad = hid_grad * silu_val
    both = jnp.concatenate([gate_grad, up_grad], 1)
    upper, _ = half_of_row(both.shape, 0)
    both = jnp.concatenate([jnp.where(upper, 0.0, both), jnp.where(upper, both, 0.0)], 1)
    both = both.astype(BF16)
    upper, _ = half_of_row((HID, ROWS), 1)
    for i, value in enumerate((gate_grad, up_grad, hidden)):
        turned = value.T
        turned_ref[i * HID : (i + 1) * HID, :] = jnp.where(upper, 0.0, turned).astype(BF16)
        turned_ref[(i + 3) * HID : (i + 4) * HID, :] = jnp.where(upper, turned, 0.0).astype(BF16)
    spans = tuple(zip(pieces, (0, 7, 15, 17, 24), (7, 15, 17, 24, 32)))
    for part in range(PARTS):
        columns_of = slice(part * HALF // PARTS, (part + 1) * HALF // PARTS)
        for h in range(2):
            base = 3 * HID * h
            proj = jnp.dot(
                turned_ref[base : base + 2 * HID, :],
                slots[:, columns_of],
                preferred_element_type=F32,
            )
            down = jnp.dot(
                turned_ref[base + 2 * HID : base + 3 * HID, :],
                slots[:, HALF + columns_of.start : HALF + columns_of.stop],
                preferred_element_type=F32,
            )
            for i in range(HALF // PARTS // 128):
                block = columns_of.start // 128 + i + h * (BLOCKS // 2)
                keep = info_ref[block].astype(F32)
                place = info_ref[BLOCKS + block]
                lanes = slice(i * 128, i * 128 + 128)
                staged[block, : 2 * HID, :] = (proj[:, lanes] * keep).astype(BF16)
                staged[block, 2 * HID :, :] = (down[:, lanes] * keep).astype(BF16)

                def send(ref, first):
                    pltpu.make_async_copy(
                        staged.at[block], ref.at[place - first], out_sems.at[block]
                    ).start()

                for ref, first, last in spans:
                    pl.when((place >= first) & (place < last))(
                        functools.partial(send, ref, first)
                    )
    copies = []
    for part in range(GRAD_PARTS):
        count = BLOCKS // 2 // GRAD_PARTS
        matching = [
            stack_rows(table_ref, weights, count * part + BLOCKS // 2 * h, count, 0, 2 * HID)
            for h in range(2)
        ]
        at = pl.ds(part * count * 128, count * 128)
        grads[:, at] = lax.dot_general(
            both,
            jnp.concatenate(matching, 1),
            (((1,), (1,)), ((), ())),
            preferred_element_type=F32,
        ).astype(BF16)
        copies.append(
            pltpu.make_async_copy(grads.at[:, at], slot_grad_ref.at[:, at], grad_sems.at[part])
        )
        copies[-1].start()
    for copy in copies:
        copy.wait()
    for block in range(BLOCKS):
        pltpu.make_async_copy(staged.at[block], pieces[0].at[0], out_sems.at[block]).wait()


def combine_kernel(back_ref, slots_ref, out_ref):
    step = pl.program_id(0)
    total = jnp.dot(back_ref[...], slots_ref[...], preferred_element_type=F32).astype(BF16)
    at = pl.multiple_of(step * COLS, COLS)
    out_ref[:, pl.ds(at, COLS)] = total[:TOK, :]
    out_ref[:, pl.ds(pl.multiple_of(at + HALF, COLS), COLS)] = total[TOK:, :]


def whole(shape):
    return pl.BlockSpec(shape, lambda i, *_: (0,) * len(shape))


def columns(rows, at=lambda i: i):
    return pl.BlockSpec((rows, COLS), lambda i, *_: (0, at(i)))


def call(kernel, steps, ins, outs, shapes, flops, nbytes, scratch=(), prefetch=0):
    return pl.pallas_call(
        kernel,
        grid_spec=pltpu.PrefetchScalarGridSpec(
            num_scalar_prefetch=prefetch,
            grid=(steps,),
            in_specs=ins,
            out_specs=outs,
            scratch_shapes=list(scratch),
        ),
        out_shape=shapes,
        compiler_params=pltpu.CompilerParams(dimension_semantics=("arbitrary",)),
        cost_estimate=pl.CostEstimate(flops=flops, bytes_accessed=nbytes, transcendentals=0),
    )


def sds(shape, dtype):
    return jax.ShapeDtypeStruct(shape, dtype)


def exchange(rows):
    return lax.all_to_all(
        rows.reshape(EXPERTS, 2 * CAP, -1), "exp", split_axis=0, concat_axis=0, tiled=True
    ).reshape(rows.shape)


def hop(value, distance):
    reps = lax.axis_size("rep")
    turn = [
        (i, (i + 2 * distance) % reps if i % 2 == 0 else (i - 2 * distance) % reps)
        for i in range(reps)
    ]
    return lax.ppermute(value, "rep", turn)


def swap(value):
    return lax.ppermute(value, "rep", [(i, i ^ 1) for i in range(lax.axis_size("rep"))])


def places(rep, sign):
    block = jnp.arange(BLOCKS, dtype=jnp.int32)
    core = rep & 1
    kind = block & 1
    ahead = (sign * ((block >> 1) - (rep >> 1))) & 15
    carrier = jnp.where(ahead == 8, kind, (ahead > 8).astype(jnp.int32))
    carrier = jnp.where(ahead == 0, core, carrier)
    distance = jnp.where(ahead > 8, 16 - ahead, ahead)
    odd = (distance & 1) == 1
    step = jnp.where(odd, distance, distance - 1)
    second = (kind != carrier).astype(jnp.int32)
    pair = 2 * ((step & 2) + ((step >> 2) & 1)) + second
    return distance == 0, odd, pair, second, carrier == core


def gathered_places(rep):
    here, odd, pair, second, local = places(rep, -1)
    at = jnp.where(here, second, jnp.where(odd, 2, 10) + pair)
    return jnp.where(local, at, at + 16)


def scattered_places(rep):
    here, odd, pair, second, local = places(rep, 1)
    at = jnp.where(here, 15 + second, jnp.where(odd, 7, 0) + pair)
    return jnp.where(local, at, at + 17)


def gather_weights(own):
    near = jnp.stack([own, swap(own)])
    one = hop(near, 1)
    five = hop(one, 4)
    three_seven = hop(jnp.concatenate([one, five]), 2)
    odd = jnp.concatenate([one, five, three_seven])
    even = hop(odd, 1)
    return near, odd, even, swap(odd), swap(even)


def add(*parts):
    return functools.reduce(jnp.add, [part.astype(F32) for part in parts])


def scatter_sum(even, odd, give_odd):
    one = hop(even, 1)
    got = swap(give_odd)
    last = lax.pad(one, jnp.zeros((), BF16), ((-4, 1, 0), (0, 0, 0), (0, 0, 0)))
    second = add(odd[4:], got[4:], last).astype(BF16)
    two = hop(second, 2)
    five = hop(add(odd[2:4], got[2:4], one[2:4], two[2:]).astype(BF16), 5)
    return five, hop(add(odd[:2], got[:2], one[:2], two[:2]).astype(BF16), 1)


def per_device(tokens, grad_out, gates, expert_ids, w_all, touched):
    rep = lax.axis_index("rep")
    ids = expert_ids.T
    mbytes = 1 << 20
    in_place = [pl.BlockSpec(memory_space=pl.ANY)]
    sent = call(
        place_kernel,
        1,
        [whole((2, TOK)), whole((2, TOK))] + in_place * 2,
        in_place[0],
        sds((ROWS, WIDTH), BF16),
        4 * ROWS * 256 * HALF,
        8 * mbytes,
        [
            pltpu.VMEM((TOK, WIDTH), BF16),
            pltpu.VMEM((TOK, WIDTH), BF16),
            pltpu.VMEM((ROWS, WIDTH), BF16),
            pltpu.SemaphoreType.DMA((2,)),
            pltpu.SemaphoreType.DMA((2 * PLACE_PARTS,)),
        ],
    )(ids, gates.T, tokens, grad_out)
    received = exchange(sent)
    back = call(
        back_kernel,
        1,
        [whole((2, TOK))],
        whole((2 * TOK, ROWS)),
        sds((2 * TOK, ROWS), BF16),
        0,
        mbytes,
    )(ids)
    gathered = gather_weights(w_all[0])
    weights = [
        pltpu.VMEM((sum(piece.shape[0] for piece in gathered), 128, 3 * HID), BF16),
        pltpu.SemaphoreType.DMA((len(gathered),)),
    ]
    table = gathered_places(rep)
    info = jnp.concatenate([touched.reshape(-1), scattered_places(rep)])
    shares = [(n, 3 * HID, 128) for n in (7, 8, 2, 7, 8)]
    slot_grad, even, odd, here, give_even, give_odd = call(
        expert_kernel,
        1,
        in_place * 6,
        in_place * 6,
        [sds((ROWS, HALF), BF16)] + [sds(share, BF16) for share in shares],
        2 * ROWS * HALF * 16 * HID,
        16 * mbytes,
        [
            pltpu.VMEM((ROWS, WIDTH), BF16),
            weights[0],
            pltpu.VMEM((6 * HID, ROWS), BF16),
            pltpu.VMEM((BLOCKS, 3 * HID, 128), BF16),
            pltpu.VMEM((ROWS, HALF), BF16),
            pltpu.SemaphoreType.DMA((2,)),
            weights[1],
            pltpu.SemaphoreType.DMA((BLOCKS,)),
            pltpu.SemaphoreType.DMA((GRAD_PARTS,)),
        ],
        2,
    )(table, info, received, *gathered)
    paired = (even.astype(F32) + swap(give_even).astype(F32)).astype(BF16)
    final = scatter_sum(paired, odd, give_odd)
    returned = exchange(slot_grad)
    token_grad = call(
        combine_kernel,
        STEPS,
        [whole((2 * TOK, ROWS)), columns(ROWS)],
        whole((TOK, WIDTH)),
        sds((TOK, WIDTH), BF16),
        2 * ROWS * 256 * HALF,
        4 * mbytes,
    )(back, returned)
    final, token_grad = lax.optimization_barrier((final, token_grad))
    total = add(here, *final)
    owned = total[:1] + swap(total[1:].astype(BF16)).astype(F32)
    return (token_grad, jnp.swapaxes(owned, 1, 2))


def solution(mesh):
    in_specs = (
        P(("rep", "exp"), None),
        P(("rep", "exp"), None),
        P(("rep", "exp"), None),
        P(("rep", "exp"), None),
        P("exp", "rep", None),
        P("rep", "exp", None),
    )
    out_specs = (P(("rep", "exp"), None), P("exp", "rep", None))

    return jax.shard_map(
        per_device, mesh=mesh, in_specs=in_specs, out_specs=out_specs, check_vma=False
    )
```
